128 devices in a mesh: rows: 8 (over x, core), cols: 16 (over y, z).
Axes of the slice: x: 4, y: 4, z: 4, core: 2. Of those that a mesh axis runs over, the one named last changes fastest.
Arguments:
- cells: int32 [1024], replicated, may hold values from 0 to 65535, as said below
- gram_slots: float32 [6, 4096, 2048], P(None, 'rows', 'cols'), may hold values from -6 to 6
- diag_inverse: float32 [2, 4096, 4096], P(None, 'rows', 'cols'), may hold values from -1 to 2.1, as said below
- lower_block: float32 [4096, 4096], P('rows', 'cols'), may hold values from -0.09375 to 0.09375
- trail_factor: float32 [4, 2, 4096, 4096], P(None, None, 'rows', 'cols'), may hold values from -0.0625 to 0.0625
Outputs:
- y_panels: float32 [2, 4096, 1024], P(None, 'rows')
- g_trail: float32 [4, 4096, 1024], P(None, 'rows', 'cols')
The draws below stay inside these ranges and needn't reach their ends.
Inputs may be any that keep to these rules, and one draw needn't show every extreme that they name: Within each aligned run of 64 list positions no column block owns more than 8 cells; one column block owns exactly 8 in every run, and so 128 listed cells in all, and no column block owns more than 128. `diag_inverse`: each matrix is lower triangular with a positive diagonal.
All inputs are finite; a program needn't handle non-finite values.
Results may differ from the reference program's by a relative error of at most 0.00011.
Values sent between devices are 32-bit elements; how exact they have to be, the bound alone decides.
No kernel may reach another device: no remote copies, remote signals or barrier semaphores. Data moves between devices by JAX's collectives and lax.ppermute only.
A program may use at most 128 MiB of HBM per device.

```python
import math
import jax
import jax.numpy as jnp
from jax import lax

P_SIZE = 4096
K = 1024
TB = 4
OWN_CELLS = 4096
CAP = 128
SLOTS = 2048
BLOCK_LIST = 64
N_COLS = 16


def draw_cells(key, part):
    owner_count = K // BLOCK_LIST
    per_owner = BLOCK_LIST // owner_count
    key_hot, key_cold, key_order, key_offset = jax.random.split(key, 4)
    hottest = jax.random.randint(key_hot, (), 0, owner_count)
    coldest = (hottest + jax.random.randint(key_cold, (owner_count,), 1, owner_count)) % owner_count
    drawn = jnp.arange(BLOCK_LIST, dtype=jnp.int32) // per_owner
    owners = jnp.where(drawn[None, :] == coldest[:, None], hottest, drawn[None, :])
    orders = jax.vmap(lambda subkey: jax.random.permutation(subkey, BLOCK_LIST))(jax.random.split(key_order, owner_count))
    shuffled = jnp.take_along_axis(owners, orders, axis=1)
    offsets = jax.random.randint(key_offset, (owner_count, BLOCK_LIST), 0, OWN_CELLS)
    return (shuffled * OWN_CELLS + offsets).reshape(K).astype(jnp.int32)


def draw_diag_inverse(key, part):
    key_off, key_diag = jax.random.split(key, 2)
    positions = jnp.arange(P_SIZE)
    below = positions[:, None] > positions[None, :]
    spread = jax.random.normal(key_off, (2, P_SIZE, P_SIZE), jnp.float32)
    diagonal = jnp.exp(jax.random.uniform(key_diag, (2, P_SIZE), jnp.float32, -0.7, 0.7))
    lower_part = jnp.where(below[None], spread * (0.8 / math.sqrt(P_SIZE)), 0.0)
    on_diag = (positions[:, None] == positions[None, :])[None]
    return (lower_part + jnp.where(on_diag, diagonal[:, :, None], 0.0)).astype(jnp.float32)


def levels(own_key, extent, cuts, least, top_value):
    def one(axis_at, shards_of):
        heights = jax.random.uniform(jax.random.fold_in(jax.random.fold_in(own_key, 6), axis_at), (shards_of,), jnp.float32, least / len(cuts), top_value / len(cuts))
        return jnp.repeat(jnp.exp(heights), extent[axis_at] // shards_of).reshape((-1,) + (1,) * (len(extent) - axis_at - 1))

    level = one(*cuts[0])
    for cut in cuts[1:]:
        level = level * one(*cut)
    return level


def noise(key, shape, width, most, cuts=(), held_as=jnp.bfloat16):
    result = jax.random.normal(key, shape, jnp.float32) * width
    if len(cuts) > 0:
        result = levels(key, shape, cuts, -0.22, 0.18) * result
    return jnp.clip(result, min=-most, max=most).astype(held_as)


def setup_inputs(seed: int = 0) -> dict:
    splits = jax.random.split(jax.random.key(seed), 6)
    cells = draw_cells(jax.random.fold_in(splits[5], 71), 0)
    gram_slots = noise(splits[1], (2 + TB, P_SIZE, SLOTS), 1.0, 6.0, ((1, 8), (2, 16)), jnp.float32)
    diag_inverse = draw_diag_inverse(jax.random.fold_in(splits[5], 71), 0)
    lower_block = noise(splits[3], (P_SIZE, P_SIZE), P_SIZE ** -0.5, 0.09375, ((0, 8), (1, 16)), jnp.float32)
    trail_factor = noise(splits[4], (TB, 2, P_SIZE, P_SIZE), (2 * P_SIZE) ** -0.5, 0.0625, ((2, 8), (3, 16)), jnp.float32)
    return dict(cells=cells, gram_slots=gram_slots, diag_inverse=diag_inverse, lower_block=lower_block, trail_factor=trail_factor)


def slot_table(cells):
    owners = (cells // OWN_CELLS).astype(jnp.int32)
    onehot = (owners[:, None] == jnp.arange(N_COLS, dtype=jnp.int32)[None, :]).astype(jnp.int32)
    before = jnp.cumsum(onehot, axis=0) - onehot
    slots_of = jnp.sum(before * onehot, axis=1).astype(jnp.int32)
    return owners, slots_of


def reference(cells, gram_slots, diag_inverse, lower_block, trail_factor):
    highest = lax.Precision.HIGHEST
    owners, slots_of = slot_table(cells)
    gram_cols = jnp.take(gram_slots, (owners * CAP + slots_of).astype(jnp.int32), axis=2)
    first_panel = jnp.dot(diag_inverse[0], gram_cols[0], precision=highest, preferred_element_type=jnp.float32)
    second_rhs = gram_cols[1] - jnp.dot(lower_block, first_panel, precision=highest, preferred_element_type=jnp.float32)
    second_panel = jnp.dot(diag_inverse[1], second_rhs, precision=highest, preferred_element_type=jnp.float32)
    solved = jnp.stack([first_panel, second_panel])
    update = jnp.einsum("tprc,pck->trk", trail_factor, solved, precision=highest, preferred_element_type=jnp.float32)
    return solved, gram_cols[2:] - update
```

```python
import jax
import jax.numpy as jnp
from jax import lax
from jax.sharding import PartitionSpec as P

NCELL = 65536
HIGHEST = lax.Precision.HIGHEST
HIGH = lax.Precision.HIGH
F32 = jnp.float32


def dot(a, b, dims, precision):
    return lax.dot_general(a, b, (dims, ((), ())), precision=precision, preferred_element_type=F32)


def body(cells, gram_slots, diag_inverse, lower_block, trail_factor):
    n_cols = lax.axis_size("cols")
    n_rows = lax.axis_size("rows")
    col = lax.axis_index("cols")
    row = lax.axis_index("rows")
    list_len = cells.shape[0]
    run_len = list_len // n_cols
    slab = list_len // n_rows
    runs_in_slab = slab // run_len
    block_rows = gram_slots.shape[1]
    capacity = gram_slots.shape[2]
    per_run = capacity // n_cols
    slab_slots = runs_in_slab * per_run
    width = diag_inverse.shape[2]
    trail_blocks = trail_factor.shape[0]
    panel_rows = block_rows * n_rows

    owners = cells // (NCELL // n_cols)
    onehot = (owners[:, None] == jnp.arange(n_cols, dtype=jnp.int32)[None, :]).astype(jnp.int32)
    blocked = onehot.reshape(n_cols, run_len, n_cols)
    lower = jnp.tril(jnp.ones((run_len, run_len), F32), -1)
    in_run = jnp.einsum("ij,bjo->bio", lower, blocked.astype(F32)).astype(jnp.int32)
    run_total = jnp.sum(blocked, axis=1)
    before = jnp.sum(
        jnp.where(
            jnp.arange(n_cols)[:, None, None] > jnp.arange(n_cols)[None, :, None],
            run_total[None, :, :],
            0,
        ),
        axis=1,
    )
    pair_rank = jnp.sum(in_run * blocked, axis=2).reshape(list_len)
    slots_of = pair_rank + jnp.sum(before[:, None, :] * blocked, axis=2).reshape(list_len)
    mine = owners == col
    position = jnp.arange(list_len, dtype=jnp.int32) // run_len * per_run + pair_rank
    slot_range = jnp.arange(capacity, dtype=jnp.int32)
    to_list = ((slots_of[None, :] == slot_range[:, None]) & mine[None, :]).astype(F32)
    to_runs = dot(
        ((position[None, :] == slot_range[:, None]) & mine[None, :]).astype(F32),
        to_list,
        ((1,), (1,)),
        lax.Precision.DEFAULT,
    )

    outgoing = lax.dot_general(
        to_runs, gram_slots[0:2], (((1,), (2,)), ((), ())), precision=HIGHEST, preferred_element_type=F32
    )
    outgoing = outgoing.reshape(n_rows, slab_slots, 2, block_rows)
    slab_gram = lax.all_to_all(outgoing, "rows", 0, 0, tiled=True)
    halves = block_rows // width
    first_gram = slab_gram[:, :, 0].reshape(n_rows, slab_slots, halves, width)
    first_gram = first_gram.transpose(0, 2, 1, 3).reshape(n_cols, slab_slots, width)
    first_gram = lax.all_to_all(first_gram, "cols", 0, 0, tiled=True).reshape(n_cols * slab_slots, width)

    slab_owner = lax.dynamic_slice_in_dim(owners, row * slab, slab)
    slab_rank = lax.dynamic_slice_in_dim(pair_rank, row * slab, slab)
    slab_slot = jnp.arange(slab, dtype=jnp.int32) // run_len * per_run + slab_rank
    from_owner = (
        jnp.arange(n_cols * slab_slots, dtype=jnp.int32)[:, None] == (slab_owner * slab_slots + slab_slot)[None, :]
    ).astype(F32)
    own_part = (
        (jnp.arange(slab_slots, dtype=jnp.int32)[:, None] == slab_slot[None, :]) & (slab_owner == col)[None, :]
    ).astype(F32)
    rhs = dot(first_gram, from_owner, ((0,), (0,)), HIGHEST)
    second_gram = lax.dot_general(
        slab_gram[:, :, 1], own_part, (((1,), (0,)), ((), ())), precision=HIGHEST, preferred_element_type=F32
    ).reshape(panel_rows, slab)

    def columns_of(block):
        return lax.all_gather(block, "rows", axis=0, tiled=True)

    inverse_0 = columns_of(diag_inverse[0])
    below = columns_of(lower_block)
    inverse_1 = columns_of(diag_inverse[1])

    def reduce_cols(partial_sum):
        terms = lax.all_to_all(partial_sum.reshape(n_cols, width, slab), "cols", 0, 0, tiled=True)
        return jnp.sum(terms, axis=0)

    def all_slabs(block):
        spread = jnp.broadcast_to(block[None], (n_rows, width, slab))
        return lax.all_to_all(spread, "rows", 0, 0, tiled=True)

    swap = [
        (r * n_cols + c, (c // 2) * n_cols + 2 * r + c % 2) for r in range(n_rows) for c in range(n_cols)
    ]

    def solution_rows(block):
        piece = lax.ppermute(block, ("rows", "cols"), swap)
        return lax.all_gather(piece, "cols", axis=0, tiled=False)

    def as_rows(pieces):
        pieces = pieces.reshape(n_rows, halves, width, slab).transpose(1, 2, 0, 3)
        return pieces.reshape(block_rows, list_len)

    first = reduce_cols(dot(inverse_0, rhs, ((1,), (0,)), HIGH))
    first_out = solution_rows(first)
    first_all = all_slabs(first)
    second_rhs = reduce_cols(second_gram - dot(below, first, ((1,), (0,)), HIGH))
    second = reduce_cols(dot(inverse_1, second_rhs, ((1,), (0,)), HIGH))
    second_all = all_slabs(second)

    trail_gram = lax.dot_general(
        gram_slots[2:], to_list, (((2,), (0,)), ((), ())), precision=HIGHEST, preferred_element_type=F32
    )
    first_trail = jnp.einsum("trc,scp->trsp", trail_factor[:, 0], first_all, precision=HIGH, preferred_element_type=F32)
    second_trail = jnp.einsum("trc,scp->trsp", trail_factor[:, 1], second_all, precision=HIGH, preferred_element_type=F32)
    terms = trail_gram - first_trail.reshape(trail_gram.shape) - second_trail.reshape(trail_gram.shape)
    trail_out = lax.psum_scatter(terms, "cols", scatter_dimension=2, tiled=True)
    second_piece = lax.ppermute(second, ("rows", "cols"), swap)
    second_out = lax.all_to_all(
        jnp.broadcast_to(second_piece[None], (n_cols, width, slab)), "cols", 0, 0, tiled=True
    )
    return jnp.stack([as_rows(first_out), as_rows(second_out)]), trail_out


def solution(mesh):
    return jax.shard_map(
        body,
        mesh=mesh,
        in_specs=(
            P(),
            P(None, "rows", "cols"),
            P(None, "rows", "cols"),
            P("rows", "cols"),
            P(None, None, "rows", "cols"),
        ),
        out_specs=(P(None, "rows", None), P(None, "rows", "cols")),
        check_vma=False,
    )
```

```python
import jax
import jax.numpy as jnp
from jax import lax
from jax.sharding import Mesh
from jax.sharding import PartitionSpec as P

NCELL = 65536
ROWS = ("x", "core")
COLS = ("y", "z")
HIGHEST = lax.Precision.HIGHEST
HIGH = lax.Precision.HIGH
F32 = jnp.float32


def dot(a, b, dims, precision):
    return lax.dot_general(a, b, (dims, ((), ())), precision=precision, preferred_element_type=F32)


def shift(value, axis, by):
    size = lax.axis_size(axis)
    return lax.ppermute(value, axis, [(i, (i + by) % size) for i in range(size)])


def exchange(value, axes):
    return lax.all_to_all(value, axes, 0, 0, tiled=True)


def spread(value, axes):
    return exchange(jnp.broadcast_to(value[None], (lax.axis_size(axes), *value.shape)), axes)


def body(cells, gram_slots, diag_inverse, lower_block, trail_factor):
    n_x, n_core, n_y, n_z = (lax.axis_size(a) for a in ROWS + COLS)
    n_rows, n_cols = n_x * n_core, n_y * n_z
    col = lax.axis_index(COLS)
    row = lax.axis_index(ROWS)
    core = lax.axis_index("core")
    x_at = lax.axis_index("x")
    list_len = cells.shape[0]
    run_len = list_len // n_cols
    slab = list_len // n_rows
    runs_in_slab = slab // run_len
    block_rows = gram_slots.shape[1]
    capacity = gram_slots.shape[2]
    per_run = capacity // n_cols
    slab_slots = runs_in_slab * per_run
    width = diag_inverse.shape[2]
    trail_blocks = trail_factor.shape[0]
    quarter = block_rows // n_z
    sub = n_core * quarter
    band = width * n_z

    owners = cells // (NCELL // n_cols)
    onehot = (owners[:, None] == jnp.arange(n_cols, dtype=jnp.int32)[None, :]).astype(jnp.int32)
    blocked = onehot.reshape(n_cols, run_len, n_cols)
    lower = jnp.tril(jnp.ones((run_len, run_len), F32), -1)
    in_run = jnp.einsum("ij,bjo->bio", lower, blocked.astype(F32)).astype(jnp.int32)
    run_total = jnp.sum(blocked, axis=1)
    runs = jnp.arange(n_cols)
    before = jnp.sum(jnp.where(runs[:, None, None] > runs[None, :, None], run_total[None, :, :], 0), axis=1)
    pair_rank = jnp.sum(in_run * blocked, axis=2).reshape(list_len)
    slots_of = pair_rank + jnp.sum(before[:, None, :] * blocked, axis=2).reshape(list_len)
    mine = owners == col
    position = jnp.arange(list_len, dtype=jnp.int32) // run_len * per_run + pair_rank
    slot_range = jnp.arange(capacity, dtype=jnp.int32)
    to_list = ((slots_of[None, :] == slot_range[:, None]) & mine[None, :]).astype(F32)
    to_runs = dot(
        ((position[None, :] == slot_range[:, None]) & mine[None, :]).astype(F32),
        to_list,
        ((1,), (1,)),
        lax.Precision.DEFAULT,
    )

    def by_quarter(matrix):
        return exchange(matrix.reshape(n_z, quarter, width), "z").transpose(1, 0, 2).reshape(quarter, band)

    def all_rows(matrix):
        return lax.all_gather(by_quarter(matrix), ROWS, axis=0, tiled=True)

    inverse_0 = all_rows(diag_inverse[0])

    outgoing = lax.dot_general(
        to_runs, gram_slots[0:2], (((1,), (2,)), ((), ())), precision=HIGHEST, preferred_element_type=F32
    )
    slab_gram = exchange(outgoing.reshape(n_rows, slab_slots, 2, block_rows), ROWS)
    slab_gram = slab_gram.reshape(n_y, n_core, slab_slots, 2, n_z, quarter).transpose(0, 4, 2, 3, 1, 5)
    sub_gram = exchange(slab_gram.reshape(n_cols, slab_slots, 2 * sub), COLS)
    slab_owner = lax.dynamic_slice_in_dim(owners, row * slab, slab)
    slab_rank = lax.dynamic_slice_in_dim(pair_rank, row * slab, slab)
    slab_slot = jnp.arange(slab, dtype=jnp.int32) // run_len * per_run + slab_rank
    from_owner = (
        jnp.arange(n_cols * slab_slots, dtype=jnp.int32)[:, None] == (slab_owner * slab_slots + slab_slot)[None, :]
    ).astype(F32)
    rhs = dot(sub_gram.reshape(n_cols * slab_slots, 2 * sub), from_owner, ((0,), (0,)), HIGHEST)
    rhs = rhs.reshape(2, sub, slab)

    below = all_rows(lower_block)
    inverse_1 = all_rows(diag_inverse[1])

    def in_order(pieces):
        lead = pieces.shape[:-3]
        pieces = pieces.reshape(*lead, n_z, n_core, quarter, slab)
        return jnp.swapaxes(pieces, -4, -3).reshape(*lead, band, slab)

    def product(matrix, operand):
        terms = dot(matrix, operand, ((1,), (0,)), HIGH).reshape(n_y, sub, slab)
        return jnp.sum(exchange(terms, "y"), axis=0)

    axes = ROWS + COLS
    sizes = (n_x, n_core, n_y, n_z)

    def device(x, k, y, z):
        return ((x * n_core + k) * n_y + y) * n_z + z

    def solution_rows(block):
        pieces = block.reshape(n_core, quarter, slab)
        moved = []
        for m in range(n_core):
            to = [
                (device(x, k, y, z), device(y, k ^ m, x, z))
                for x in range(n_x)
                for k in range(n_core)
                for y in range(n_y)
                for z in range(n_z)
            ]
            moved.append(lax.ppermute(lax.dynamic_index_in_dim(pieces, core ^ m, 0, keepdims=False), axes, to))
        piece = jnp.where(core == 0, jnp.concatenate(moved, axis=1), jnp.concatenate(moved[::-1], axis=1))
        return lax.all_gather(piece, COLS, axis=0, tiled=False)

    def as_rows(pieces):
        pieces = pieces.reshape(n_y, n_z, quarter, n_core * slab).transpose(1, 2, 0, 3)
        return pieces.reshape(block_rows, list_len)

    first = product(inverse_0, in_order(spread(rhs[0], "z")))
    first_band = in_order(spread(first, "z"))
    first_out = solution_rows(first)
    second_rhs = rhs[1] - product(below, first_band)

    trail = jnp.concatenate([trail_factor[:, 0], trail_factor[:, 1], gram_slots[2:]], axis=2)
    depth = trail.shape[2]
    trail = trail.reshape(trail_blocks, n_z, quarter, depth).transpose(1, 0, 2, 3)
    trail = exchange(trail, "z")
    trail_pair = jnp.stack([trail, shift(trail, "core", 1)])
    trail_pair = trail_pair.transpose(2, 0, 3, 1, 4).reshape(trail_blocks * sub, n_z, depth)
    trail_0 = trail_pair[:, :, :width].reshape(-1, band)
    trail_1 = trail_pair[:, :, width : 2 * width].reshape(-1, band)
    trail_g = trail_pair[:, :, 2 * width :].reshape(-1, n_z * capacity)

    first_all = jnp.stack([first_band] + [shift(first_band, "x", -d) for d in range(1, n_x)])
    first_all = jnp.take(first_all, (jnp.arange(n_x) - x_at) % n_x, axis=0)
    trail_owner = col // n_z * n_z + jnp.arange(n_z, dtype=jnp.int32)
    to_lists = (
        (slots_of[None, None, :] == slot_range[None, :, None]) & (owners[None, None, :] == trail_owner[:, None, None])
    ).astype(F32)
    to_lists = to_lists.reshape(n_z * capacity, n_x, n_core, slab)
    to_lists = lax.dynamic_index_in_dim(to_lists, core, 2, keepdims=False).transpose(1, 0, 2)

    def against(matrix, lists, precision):
        return jnp.einsum("rc,xck->xrk", matrix, lists, precision=precision, preferred_element_type=F32)

    base = against(trail_g, to_lists, HIGHEST) - against(trail_0, first_all, HIGH)

    second = product(inverse_1, in_order(spread(second_rhs, "z")))
    second_out = solution_rows(second)
    second_all = in_order(spread(second, ("x", "z")).reshape(n_x, n_z, sub, slab))
    terms = base - against(trail_1, second_all, HIGH)
    total = jnp.sum(exchange(terms, "y"), axis=0).reshape(trail_blocks, n_core, quarter, slab)
    kept, given = total[:, 0], total[:, 1]
    got = shift(given, "core", 1)
    pair = jnp.where(core == 0, jnp.stack([kept, got]), jnp.stack([got, kept]))
    pair = pair.reshape(n_core, trail_blocks, quarter, n_z // n_core, run_len).transpose(0, 3, 1, 2, 4)
    out = exchange(pair.reshape(n_z, trail_blocks, quarter, run_len), "z")
    trail_out = out.transpose(1, 0, 2, 3).reshape(trail_blocks, block_rows, run_len)
    return jnp.stack([as_rows(first_out), as_rows(second_out)]), trail_out


def solution(mesh):
    n_rows, n_cols = mesh.devices.shape
    side = int(round(n_cols**0.5))
    mesh = Mesh(mesh.devices.reshape(n_rows // 2, 2, side, n_cols // side), ROWS + COLS)
    return jax.shard_map(
        body,
        mesh=mesh,
        in_specs=(
            P(),
            P(None, ROWS, COLS),
            P(None, ROWS, COLS),
            P(ROWS, COLS),
            P(None, None, ROWS, COLS),
        ),
        out_specs=(P(None, ROWS, None), P(None, ROWS, COLS)),
        check_vma=False,
    )
```

```python
import functools

import jax
import jax.numpy as jnp
from jax import lax
from jax.experimental import pallas as pl
from jax.experimental.pallas import tpu as pltpu
from jax.sharding import Mesh
from jax.sharding import PartitionSpec as P

NCELL = 65536
ROWS = ("x", "core")
COLS = ("y", "z")
HIGHEST = lax.Precision.HIGHEST
F32 = jnp.float32
BF16 = jnp.bfloat16
SMEM = pl.BlockSpec(memory_space=pltpu.SMEM)


def dot(a, b, dims, precision):
    return lax.dot_general(a, b, (dims, ((), ())), precision=precision, preferred_element_type=F32)


def shift(value, axis, by):
    size = lax.axis_size(axis)
    return lax.ppermute(value, axis, [(i, (i + by) % size) for i in range(size)])


def exchange(value, axes):
    return lax.all_to_all(value, axes, 0, 0, tiled=True)


def spread(value, axes):
    return exchange(jnp.broadcast_to(value[None], (lax.axis_size(axes), *value.shape)), axes)


def split(value):
    high = value.astype(BF16)
    return high, (value - high.astype(F32)).astype(BF16)


def mul(a, b):
    f = lambda u, v: jnp.dot(u, v, preferred_element_type=F32)
    return f(a[0], b[0]) + (f(a[0], b[1]) + f(a[1], b[0]))


def band_rows(ref, lead, at, by, n_z):
    source = lax.rem(at + n_z - by, n_z)
    per = n_z // 2
    quarters = [ref[(*lead, per * lax.rem(source, 2) + i, source // 2)] for i in range(per)]
    return jnp.concatenate(quarters, axis=0)


def product_kernel(n_z, at_ref, matrix_ref, operand_ref, out_ref):
    width = matrix_ref.shape[1] // n_z
    total = None
    for by in range(n_z):
        rows = split(band_rows(operand_ref, (), at_ref[0], by, n_z))
        term = mul(split(matrix_ref[:, by * width : (by + 1) * width]), rows)
        total = term if total is None else total + term
    out_ref[0] = total


def apply_matrix(at_z, matrix, pieces, n_y):
    rows, band = matrix.shape
    slab = pieces.shape[-1]
    return pl.pallas_call(
        functools.partial(product_kernel, pieces.shape[0]),
        grid=(n_y,),
        in_specs=[
            SMEM,
            pl.BlockSpec((rows // n_y, band), lambda i: (i, 0)),
            pl.BlockSpec(pieces.shape, lambda i: (0, 0, 0, 0)),
        ],
        out_specs=pl.BlockSpec((1, rows // n_y, slab), lambda i: (i, 0, 0)),
        out_shape=jax.ShapeDtypeStruct((n_y, rows // n_y, slab), F32),
        cost_estimate=pl.CostEstimate(
            flops=6 * rows * band * slab, bytes_accessed=4 * rows * band, transcendentals=0
        ),
    )(at_z, matrix, pieces)


def trail_kernel(n_z, n_x, with_gram, one_list, at_ref, *refs):
    lists = refs[:1] if one_list else refs[:n_x]
    refs = refs[len(lists) :]
    factor = refs[: 2 * n_z]
    refs = refs[2 * n_z :]
    gram = refs[: 2 * n_z] if with_gram else ()
    start_ref, out_ref = refs[len(gram) :]
    at_x, at_z = at_ref[0], at_ref[1]
    blocks, quarter, _ = factor[0].shape
    slab = out_ref.shape[-1]
    half = blocks * quarter
    operands = []
    for by in range(n_z):
        cols = [
            band_rows(lists[0], (i,), at_z, by, n_z) if one_list else band_rows(lists[i], (), at_z, by, n_z)
            for i in range(n_x)
        ]
        operands.append(split(jnp.concatenate(cols, axis=1)))
    for side in range(2):
        total = None
        for by in range(n_z):
            piece = factor[side * n_z + by][...]
            term = mul(split(piece.reshape(half, piece.shape[-1])), operands[by])
            total = term if total is None else total + term
        placed = None
        for by in range(n_z if with_gram else 0):
            piece = gram[side * n_z + by][...]
            high, low = split(piece.reshape(half, piece.shape[-1]))
            chosen = start_ref[lax.rem(at_z + n_z - by, n_z)]
            term = jnp.dot(high, chosen, preferred_element_type=F32) + jnp.dot(low, chosen, preferred_element_type=F32)
            placed = term if placed is None else placed + term
        for i in range(n_x):
            at = i if one_list else lax.rem(at_x + i, n_x)
            mine = slice(i * slab, (i + 1) * slab)
            into = pl.ds(side * half, half)
            first = placed[:, mine] if with_gram else start_ref[at, into, :]
            out_ref[at, into, :] = first - total[:, mine]


def apply_trail(where, own, other, which, lists, start, with_gram, n_x, slots):
    n_z = len(own)
    blocks, quarter, depth = own[0].shape
    width = (depth - slots) // 2
    slab = lists[0].shape[-1]
    whole = lambda v: pl.BlockSpec(v.shape, lambda *_: (0,) * v.ndim)
    part = pl.BlockSpec((blocks, quarter, width), lambda *_: (0, 0, which))
    pieces = [*own, *other]
    specs = [SMEM] + [whole(v) for v in lists] + [part] * (2 * n_z)
    args = [where, *lists, *pieces]
    if with_gram:
        specs += [pl.BlockSpec((blocks, quarter, slots), lambda *_: (0, 0, 2 * width // slots))] * (2 * n_z)
        args += pieces
    rows = 2 * blocks * quarter
    return pl.pallas_call(
        functools.partial(trail_kernel, n_z, n_x, with_gram, len(lists) == 1),
        grid=(1,),
        in_specs=specs + [whole(start)],
        out_specs=pl.BlockSpec((n_x, rows, slab), lambda *_: (0, 0, 0)),
        out_shape=jax.ShapeDtypeStruct((n_x, rows, slab), F32),
        cost_estimate=pl.CostEstimate(
            flops=6 * rows * n_z * width * n_x * slab, bytes_accessed=12 * 2**20, transcendentals=0
        ),
    )(*args, start)


def rows_kernel(first_ref, second_ref, out_ref):
    n_y, wide = first_ref.shape[0], first_ref.shape[-1]
    for i in range(n_y):
        out_ref[0, :, i * wide : (i + 1) * wide] = first_ref[i, 0]
        out_ref[1, :, i * wide : (i + 1) * wide] = second_ref[i, 0]


def as_rows(first, second):
    n_y, n_z, quarter, wide = first.shape
    spec = pl.BlockSpec((n_y, 1, quarter, wide), lambda i: (0, i, 0, 0))
    return pl.pallas_call(
        rows_kernel,
        grid=(n_z,),
        in_specs=[spec, spec],
        out_specs=pl.BlockSpec((2, quarter, n_y * wide), lambda i: (0, i, 0)),
        out_shape=jax.ShapeDtypeStruct((2, n_z * quarter, n_y * wide), F32),
    )(first, second)


def body(cells, gram_slots, diag_inverse, lower_block, trail_factor):
    n_x, n_core, n_y, n_z = (lax.axis_size(a) for a in ROWS + COLS)
    n_rows, n_cols = n_x * n_core, n_y * n_z
    col = lax.axis_index(COLS)
    row = lax.axis_index(ROWS)
    core = lax.axis_index("core")
    x_at = lax.axis_index("x")
    z_at = lax.axis_index("z")
    list_len = cells.shape[0]
    run_len = list_len // n_cols
    slab = list_len // n_rows
    runs_in_slab = slab // run_len
    block_rows = gram_slots.shape[1]
    capacity = gram_slots.shape[2]
    per_run = capacity // n_cols
    slab_slots = runs_in_slab * per_run
    width = diag_inverse.shape[2]
    trail_blocks = trail_factor.shape[0]
    quarter = block_rows // n_z
    sub = n_core * quarter

    owners = cells // (NCELL // n_cols)
    onehot = (owners[:, None] == jnp.arange(n_cols, dtype=jnp.int32)[None, :]).astype(jnp.int32)
    blocked = onehot.reshape(n_cols, run_len, n_cols)
    lower = jnp.tril(jnp.ones((run_len, run_len), F32), -1)
    in_run = jnp.einsum("ij,bjo->bio", lower, blocked.astype(F32)).astype(jnp.int32)
    run_total = jnp.sum(blocked, axis=1)
    runs = jnp.arange(n_cols)
    before = jnp.sum(jnp.where(runs[:, None, None] > runs[None, :, None], run_total[None, :, :], 0), axis=1)
    pair_rank = jnp.sum(in_run * blocked, axis=2).reshape(list_len)
    slots_of = pair_rank + jnp.sum(before[:, None, :] * blocked, axis=2).reshape(list_len)
    mine = owners == col
    position = jnp.arange(list_len, dtype=jnp.int32) // run_len * per_run + pair_rank
    slot_range = jnp.arange(capacity, dtype=jnp.int32)
    to_list = ((slots_of[None, :] == slot_range[:, None]) & mine[None, :]).astype(F32)
    to_runs = dot(
        ((position[None, :] == slot_range[:, None]) & mine[None, :]).astype(F32),
        to_list,
        ((1,), (1,)),
        lax.Precision.DEFAULT,
    )

    def quarters(cut):
        return [cut(z_at)] + [shift(cut((z_at + by) % n_z), "z", by) for by in range(1, n_z)]

    def rows_at(matrix, at):
        return lax.dynamic_slice_in_dim(matrix, at * quarter, quarter, matrix.ndim - 2)

    def all_rows(pieces):
        return lax.all_gather(jnp.concatenate(pieces, axis=1), ROWS, axis=0, tiled=True)

    inverse_0 = all_rows(quarters(lambda at: rows_at(diag_inverse[0], at)))
    later = quarters(lambda at: jnp.stack([rows_at(lower_block, at), rows_at(diag_inverse[1], at)]))

    outgoing = lax.dot_general(
        to_runs, gram_slots[0:2], (((1,), (2,)), ((), ())), precision=HIGHEST, preferred_element_type=F32
    )
    slab_gram = exchange(outgoing.reshape(n_rows, slab_slots, 2, block_rows), ROWS)
    slab_gram = slab_gram.reshape(n_y, n_core, slab_slots, 2, n_z, quarter).transpose(0, 4, 2, 3, 1, 5)
    sub_gram = exchange(slab_gram.reshape(n_cols, slab_slots, 2 * sub), COLS)
    slab_owner = lax.dynamic_slice_in_dim(owners, row * slab, slab)
    slab_rank = lax.dynamic_slice_in_dim(pair_rank, row * slab, slab)
    slab_slot = jnp.arange(slab, dtype=jnp.int32) // run_len * per_run + slab_rank
    from_owner = (
        jnp.arange(n_cols * slab_slots, dtype=jnp.int32)[:, None] == (slab_owner * slab_slots + slab_slot)[None, :]
    ).astype(F32)
    rhs = dot(sub_gram.reshape(n_cols * slab_slots, 2 * sub), from_owner, ((0,), (0,)), HIGHEST)
    rhs = rhs.reshape(2, sub, slab)

    below = all_rows([v[0] for v in later])
    inverse_1 = all_rows([v[1] for v in later])
    where_z = z_at.astype(jnp.int32).reshape(1)

    def spread_z(block):
        return spread(block, "z").reshape(n_z, n_core, quarter, slab)

    def product(matrix, pieces):
        return jnp.sum(exchange(apply_matrix(where_z, matrix, pieces, n_y), "y"), axis=0)

    axes = ROWS + COLS
    sizes = (n_x, n_core, n_y, n_z)

    def device(x, k, y, z):
        return ((x * n_core + k) * n_y + y) * n_z + z

    def solution_rows(block):
        pieces = block.reshape(n_core, quarter, slab)
        moved = []
        for m in range(n_core):
            to = [
                (device(x, k, y, z), device(y, k ^ m, x, z))
                for x in range(n_x)
                for k in range(n_core)
                for y in range(n_y)
                for z in range(n_z)
            ]
            moved.append(lax.ppermute(lax.dynamic_index_in_dim(pieces, core ^ m, 0, keepdims=False), axes, to))
        piece = jnp.where(core == 0, jnp.concatenate(moved, axis=1), jnp.concatenate(moved[::-1], axis=1))
        return lax.all_gather(piece, COLS, axis=0, tiled=False)

    first = product(inverse_0, spread_z(rhs[0]))
    first_pieces = spread_z(first)
    first_out = solution_rows(first)
    second_rhs = rhs[1] - product(below, first_pieces)

    factor, trail_gram, _ = lax.optimization_barrier((trail_factor, gram_slots[2:], rhs))
    own = quarters(
        lambda at: jnp.concatenate(
            [rows_at(factor[:, 0], at), rows_at(factor[:, 1], at), rows_at(trail_gram, at)], axis=2
        )
    )
    other = [shift(v, "core", 1) for v in own]
    trail_owner = col // n_z * n_z + jnp.arange(n_z, dtype=jnp.int32)
    slab_order = ((x_at + jnp.arange(n_x, dtype=jnp.int32)) % n_x * n_core + core)[:, None] * slab
    list_order = (slab_order + jnp.arange(slab, dtype=jnp.int32)[None, :]).reshape(-1)
    core_lists = lambda v: jnp.take(v, list_order)
    to_lists = (
        (core_lists(slots_of)[None, None, :] == slot_range[None, :, None])
        & (core_lists(owners)[None, None, :] == trail_owner[:, None, None])
    ).astype(BF16)
    where = jnp.stack([x_at, z_at]).astype(jnp.int32)
    first_all = [first_pieces] + [shift(first_pieces, "x", -d) for d in range(1, n_x)]
    base = apply_trail(where, own, other, 0, first_all, to_lists, True, n_x, capacity)

    second = product(inverse_1, spread_z(second_rhs))
    second_out = solution_rows(second)
    second_all = spread(second, ("x", "z")).reshape(n_x, n_z, n_core, quarter, slab)
    terms = apply_trail(where, own, other, 1, [second_all], base, False, n_x, capacity)
    total = jnp.sum(exchange(terms, "y"), axis=0).reshape(n_core, trail_blocks, quarter, slab)
    kept, given = total[0], total[1]
    got = shift(given, "core", 1)
    pair = jnp.where(core == 0, jnp.stack([kept, got]), jnp.stack([got, kept]))
    pair = pair.reshape(n_core, trail_blocks, quarter, n_z // n_core, run_len).transpose(0, 3, 1, 2, 4)
    out = exchange(pair.reshape(n_z, trail_blocks, quarter, run_len), "z")
    trail_out = out.transpose(1, 0, 2, 3).reshape(trail_blocks, block_rows, run_len)
    return as_rows(*(v.reshape(n_y, n_z, quarter, n_core * slab) for v in (first_out, second_out))), trail_out


def solution(mesh):
    n_rows, n_cols = mesh.devices.shape
    side = int(round(n_cols**0.5))
    mesh = Mesh(mesh.devices.reshape(n_rows // 2, 2, side, n_cols // side), ROWS + COLS)
    return jax.shard_map(
        body,
        mesh=mesh,
        in_specs=(
            P(),
            P(None, ROWS, COLS),
            P(None, ROWS, COLS),
            P(ROWS, COLS),
            P(None, None, ROWS, COLS),
        ),
        out_specs=(P(None, ROWS, None), P(None, ROWS, COLS)),
        check_vma=False,
    )
```

```python
import functools

import jax
import jax.numpy as jnp
from jax import lax
from jax.experimental import pallas as pl
from jax.experimental.pallas import tpu as pltpu
from jax.sharding import Mesh
from jax.sharding import PartitionSpec as P

NCELL = 65536
ROWS = ("x", "core")
COLS = ("y", "z")
HIGHEST = lax.Precision.HIGHEST
F32 = jnp.float32
BF16 = jnp.bfloat16
SMEM = pl.BlockSpec(memory_space=pltpu.SMEM)


def dot(a, b, dims, precision):
    return lax.dot_general(a, b, (dims, ((), ())), precision=precision, preferred_element_type=F32)


def shift(value, axis, by):
    size = lax.axis_size(axis)
    return lax.ppermute(value, axis, [(i, (i + by) % size) for i in range(size)])


def exchange(value, axes):
    return lax.all_to_all(value, axes, 0, 0, tiled=True)


def spread(value, axes):
    return exchange(jnp.broadcast_to(value[None], (lax.axis_size(axes), *value.shape)), axes)


def split(value):
    high = value.astype(BF16)
    return high, (value - high.astype(F32)).astype(BF16)


def mul(a, b):
    f = lambda u, v: jnp.dot(u, v, preferred_element_type=F32)
    return f(a[0], b[0]) + (f(a[0], b[1]) + f(a[1], b[0]))


def band_rows(ref, lead, at, by, n_z):
    source = lax.rem(at + n_z - by, n_z)
    per = n_z // 2
    quarters = [ref[(*lead, per * lax.rem(source, 2) + i, source // 2)] for i in range(per)]
    return jnp.concatenate(quarters, axis=0)


def product_kernel(n_z, at_ref, matrix_ref, operand_ref, out_ref):
    width = matrix_ref.shape[1] // n_z
    slab = operand_ref.shape[-1]
    total = None
    for by in range(n_z):
        high, low = split(band_rows(operand_ref, (), at_ref[0], by, n_z))
        left = split(matrix_ref[:, by * width : (by + 1) * width])
        both = jnp.dot(left[0], jnp.concatenate([high, low], axis=1), preferred_element_type=F32)
        term = both[:, :slab] + (both[:, slab:] + jnp.dot(left[1], high, preferred_element_type=F32))
        total = term if total is None else total + term
    out_ref[...] = total.reshape(out_ref.shape)


def apply_matrix(at_z, matrix, pieces, n_y):
    rows, band = matrix.shape
    slab = pieces.shape[-1]
    return pl.pallas_call(
        functools.partial(product_kernel, pieces.shape[0]),
        grid=(2,),
        in_specs=[
            SMEM,
            pl.BlockSpec((rows // 2, band), lambda i: (i, 0)),
            pl.BlockSpec(pieces.shape, lambda i: (0, 0, 0, 0)),
        ],
        out_specs=pl.BlockSpec((n_y // 2, rows // n_y, slab), lambda i: (i, 0, 0)),
        out_shape=jax.ShapeDtypeStruct((n_y, rows // n_y, slab), F32),
        cost_estimate=pl.CostEstimate(
            flops=6 * rows * band * slab, bytes_accessed=4 * rows * band, transcendentals=0
        ),
    )(at_z, matrix, pieces)


def trail_kernel(n_z, n_x, with_gram, one_list, at_ref, *refs):
    lists = refs[:1] if one_list else refs[:n_x]
    refs = refs[len(lists) :]
    factor = refs[: 2 * n_z]
    refs = refs[2 * n_z :]
    gram = refs[: 2 * n_z] if with_gram else ()
    start_ref, out_ref = refs[len(gram) :]
    at_x, at_z = at_ref[0], at_ref[1]
    blocks, quarter, _ = factor[0].shape
    slab = out_ref.shape[-1]
    half = blocks * quarter
    operands = []
    for by in range(n_z):
        cols = [
            band_rows(lists[0], (i,), at_z, by, n_z) if one_list else band_rows(lists[i], (), at_z, by, n_z)
            for i in range(n_x)
        ]
        operands.append(split(jnp.concatenate(cols, axis=1)))
    for side in range(2):
        total = None
        for by in range(n_z):
            piece = factor[side * n_z + by][...]
            term = mul(split(piece.reshape(half, piece.shape[-1])), operands[by])
            total = term if total is None else total + term
        placed = None
        for by in range(n_z if with_gram else 0):
            piece = gram[side * n_z + by][...]
            high, low = split(piece.reshape(half, piece.shape[-1]))
            chosen = start_ref[lax.rem(at_z + n_z - by, n_z)]
            term = jnp.dot(high, chosen, preferred_element_type=F32) + jnp.dot(low, chosen, preferred_element_type=F32)
            placed = term if placed is None else placed + term
        for i in range(n_x):
            at = i if one_list else lax.rem(at_x + i, n_x)
            mine = slice(i * slab, (i + 1) * slab)
            into = pl.ds(side * half, half)
            first = placed[:, mine] if with_gram else start_ref[at, into, :]
            out_ref[at, into, :] = first - total[:, mine]


def apply_trail(where, own, other, width, lists, start, with_gram, n_x):
    n_z = len(own)
    blocks, quarter, depth = own[0].shape
    slots = depth - width
    slab = lists[0].shape[-1]
    whole = lambda v: pl.BlockSpec(v.shape, lambda *_: (0,) * v.ndim)
    part = pl.BlockSpec((blocks, quarter, width), lambda *_: (0, 0, 0))
    pieces = [*own, *other]
    specs = [SMEM] + [whole(v) for v in lists] + [part] * (2 * n_z)
    args = [where, *lists, *pieces]
    if with_gram:
        specs += [pl.BlockSpec((blocks, quarter, slots), lambda *_: (0, 0, width // slots))] * (2 * n_z)
        args += pieces
    rows = 2 * blocks * quarter
    return pl.pallas_call(
        functools.partial(trail_kernel, n_z, n_x, with_gram, len(lists) == 1),
        grid=(1,),
        in_specs=specs + [whole(start)],
        out_specs=pl.BlockSpec((n_x, rows, slab), lambda *_: (0, 0, 0)),
        out_shape=jax.ShapeDtypeStruct((n_x, rows, slab), F32),
        cost_estimate=pl.CostEstimate(
            flops=6 * rows * n_z * width * n_x * slab, bytes_accessed=12 * 2**20, transcendentals=0
        ),
    )(*args, start)


def rows_kernel(first_ref, second_ref, out_ref):
    n_y, wide = first_ref.shape[0], first_ref.shape[-1]
    for i in range(n_y):
        out_ref[0, :, i * wide : (i + 1) * wide] = first_ref[i, 0]
        out_ref[1, :, i * wide : (i + 1) * wide] = second_ref[i, 0]


def as_rows(first, second):
    n_y, n_z, quarter, wide = first.shape
    spec = pl.BlockSpec((n_y, 1, quarter, wide), lambda i: (0, i, 0, 0))
    return pl.pallas_call(
        rows_kernel,
        grid=(n_z,),
        in_specs=[spec, spec],
        out_specs=pl.BlockSpec((2, quarter, n_y * wide), lambda i: (0, i, 0)),
        out_shape=jax.ShapeDtypeStruct((2, n_z * quarter, n_y * wide), F32),
    )(first, second)


def after(value, *others):
    return lax.optimization_barrier((value, *others))[0]


def body(cells, gram_slots, diag_inverse, lower_block, trail_factor):
    n_x, n_core, n_y, n_z = (lax.axis_size(a) for a in ROWS + COLS)
    n_rows, n_cols = n_x * n_core, n_y * n_z
    col = lax.axis_index(COLS)
    row = lax.axis_index(ROWS)
    core = lax.axis_index("core")
    x_at = lax.axis_index("x")
    z_at = lax.axis_index("z")
    list_len = cells.shape[0]
    run_len = list_len // n_cols
    slab = list_len // n_rows
    runs_in_slab = slab // run_len
    block_rows = gram_slots.shape[1]
    capacity = gram_slots.shape[2]
    per_run = capacity // n_cols
    slab_slots = runs_in_slab * per_run
    width = diag_inverse.shape[2]
    trail_blocks = trail_factor.shape[0]
    quarter = block_rows // n_z
    sub = n_core * quarter

    owners = cells // (NCELL // n_cols)
    onehot = (owners[:, None] == jnp.arange(n_cols, dtype=jnp.int32)[None, :]).astype(jnp.int32)
    blocked = onehot.reshape(n_cols, run_len, n_cols)
    lower = jnp.tril(jnp.ones((run_len, run_len), F32), -1)
    in_run = jnp.einsum("ij,bjo->bio", lower, blocked.astype(F32)).astype(jnp.int32)
    run_total = jnp.sum(blocked, axis=1)
    runs = jnp.arange(n_cols)
    before = jnp.sum(jnp.where(runs[:, None, None] > runs[None, :, None], run_total[None, :, :], 0), axis=1)
    pair_rank = jnp.sum(in_run * blocked, axis=2).reshape(list_len)
    slots_of = pair_rank + jnp.sum(before[:, None, :] * blocked, axis=2).reshape(list_len)
    mine = owners == col
    position = jnp.arange(list_len, dtype=jnp.int32) // run_len * per_run + pair_rank
    slot_range = jnp.arange(capacity, dtype=jnp.int32)
    to_list = ((slots_of[None, :] == slot_range[:, None]) & mine[None, :]).astype(F32)
    to_runs = dot(
        ((position[None, :] == slot_range[:, None]) & mine[None, :]).astype(F32),
        to_list,
        ((1,), (1,)),
        lax.Precision.DEFAULT,
    )

    def moved(cut, by):
        return shift(cut((z_at + by) % n_z), "z", by) if by else cut(z_at)

    def quarters(cut):
        return [moved(cut, by) for by in range(n_z)]

    def rows_at(matrix, at):
        return lax.dynamic_slice_in_dim(matrix, at * quarter, quarter, matrix.ndim - 2)

    def all_rows(pieces):
        return lax.all_gather(jnp.concatenate(pieces, axis=1), ROWS, axis=0, tiled=True)

    matrices = (diag_inverse[0], lower_block, diag_inverse[1])
    pieces = quarters(lambda at: jnp.stack([rows_at(m, at) for m in matrices]))
    inverse_0, below, inverse_1 = (all_rows([v[i] for v in pieces]) for i in range(3))
    outgoing = lax.dot_general(
        to_runs, gram_slots[0:2], (((1,), (2,)), ((), ())), precision=HIGHEST, preferred_element_type=F32
    )
    slab_gram = exchange(outgoing.reshape(n_rows, slab_slots, 2, block_rows), ROWS)
    slab_gram = slab_gram.reshape(n_y, n_core, slab_slots, 2, n_z, quarter).transpose(0, 4, 2, 3, 1, 5)
    sub_gram = exchange(slab_gram.reshape(n_cols, slab_slots, 2 * sub), COLS)
    slab_owner = lax.dynamic_slice_in_dim(owners, row * slab, slab)
    slab_rank = lax.dynamic_slice_in_dim(pair_rank, row * slab, slab)
    slab_slot = jnp.arange(slab, dtype=jnp.int32) // run_len * per_run + slab_rank
    from_owner = (
        jnp.arange(n_cols * slab_slots, dtype=jnp.int32)[:, None] == (slab_owner * slab_slots + slab_slot)[None, :]
    ).astype(F32)
    rhs = dot(sub_gram.reshape(n_cols * slab_slots, 2 * sub), from_owner, ((0,), (0,)), HIGHEST)
    rhs = rhs.reshape(2, sub, slab)

    where_z = z_at.astype(jnp.int32).reshape(1)

    def spread_z(block):
        return spread(block, "z").reshape(n_z, n_core, quarter, slab)

    def product(matrix, pieces):
        return jnp.sum(exchange(apply_matrix(where_z, matrix, pieces, n_y), "y"), axis=0)

    axes = ROWS + COLS
    sizes = (n_x, n_core, n_y, n_z)

    def device(x, k, y, z):
        return ((x * n_core + k) * n_y + y) * n_z + z

    def solution_rows(block):
        pieces = block.reshape(n_core, quarter, slab)
        moved = []
        for m in range(n_core):
            to = [
                (device(x, k, y, z), device(y, k ^ m, x, z))
                for x in range(n_x)
                for k in range(n_core)
                for y in range(n_y)
                for z in range(n_z)
            ]
            moved.append(lax.ppermute(lax.dynamic_index_in_dim(pieces, core ^ m, 0, keepdims=False), axes, to))
        piece = jnp.where(core == 0, jnp.concatenate(moved, axis=1), jnp.concatenate(moved[::-1], axis=1))
        return lax.all_gather(piece, COLS, axis=0, tiled=False)

    def trail_0(at):
        return jnp.concatenate([rows_at(early[0], at), rows_at(early[1], at)], axis=2)

    def trail_1(at):
        return rows_at(late, at)

    rhs_pieces = spread_z(rhs[0])
    early = lax.optimization_barrier((trail_factor[:, 0], gram_slots[2:], rhs_pieces))
    own_0 = {by: moved(trail_0, by) for by in range(n_z) if by != n_z // 2}
    first = after(product(inverse_0, rhs_pieces), *own_0.values())
    first_pieces = spread_z(first)
    first_out = solution_rows(first)
    early = lax.optimization_barrier((trail_factor[:, 0], gram_slots[2:], first_pieces))
    own_0[n_z // 2] = moved(trail_0, n_z // 2)
    first_all = [first_pieces] + [shift(first_pieces, "x", -d) for d in range(1, n_x)]
    second_rhs = rhs[1] - product(below, first_pieces)
    second_rhs = after(second_rhs, own_0[n_z // 2], *first_all)
    second_pieces = spread_z(second_rhs)
    late = after(trail_factor[:, 1], second_pieces)
    own_0 = [own_0[by] for by in range(n_z)]
    own_1 = quarters(trail_1)
    other_0 = [shift(v, "core", 1) for v in own_0]
    other_1 = [shift(v, "core", 1) for v in own_1]

    trail_owner = col // n_z * n_z + jnp.arange(n_z, dtype=jnp.int32)
    slab_order = ((x_at + jnp.arange(n_x, dtype=jnp.int32)) % n_x * n_core + core)[:, None] * slab
    list_order = (slab_order + jnp.arange(slab, dtype=jnp.int32)[None, :]).reshape(-1)
    to_lists = (
        (jnp.take(slots_of, list_order)[None, None, :] == slot_range[None, :, None])
        & (jnp.take(owners, list_order)[None, None, :] == trail_owner[:, None, None])
    ).astype(BF16)
    where = jnp.stack([x_at, z_at]).astype(jnp.int32)
    base = apply_trail(where, own_0, other_0, width, first_all, to_lists, True, n_x)

    second = after(product(inverse_1, second_pieces), base, *own_1)
    second_out = solution_rows(second)
    second_all = spread(second, ("x", "z")).reshape(n_x, n_z, n_core, quarter, slab)
    terms = apply_trail(where, own_1, other_1, width, [second_all], base, False, n_x)
    total = jnp.sum(exchange(terms, "y"), axis=0).reshape(n_core, trail_blocks, quarter, slab)
    kept, given = total[0], total[1]
    got = shift(given, "core", 1)
    pair = jnp.where(core == 0, jnp.stack([kept, got]), jnp.stack([got, kept]))
    pair = pair.reshape(n_core, trail_blocks, quarter, n_z // n_core, run_len).transpose(0, 3, 1, 2, 4)
    out = exchange(pair.reshape(n_z, trail_blocks, quarter, run_len), "z")
    trail_out = out.transpose(1, 0, 2, 3).reshape(trail_blocks, block_rows, run_len)
    return as_rows(*(v.reshape(n_y, n_z, quarter, n_core * slab) for v in (first_out, second_out))), trail_out


def solution(mesh):
    n_rows, n_cols = mesh.devices.shape
    side = int(round(n_cols**0.5))
    mesh = Mesh(mesh.devices.reshape(n_rows // 2, 2, side, n_cols // side), ROWS + COLS)
    return jax.shard_map(
        body,
        mesh=mesh,
        in_specs=(
            P(),
            P(None, ROWS, COLS),
            P(None, ROWS, COLS),
            P(ROWS, COLS),
            P(None, None, ROWS, COLS),
        ),
        out_specs=(P(None, ROWS, None), P(None, ROWS, COLS)),
        check_vma=False,
    )
```

```python
import functools

import jax
import jax.numpy as jnp
from jax import lax
from jax.experimental import pallas as pl
from jax.experimental.pallas import tpu as pltpu
from jax.sharding import Mesh
from jax.sharding import PartitionSpec as P

NCELL = 65536
ROWS = ("x", "core")
COLS = ("y", "z")
HIGHEST = lax.Precision.HIGHEST
F32 = jnp.float32
BF16 = jnp.bfloat16
SMEM = pl.BlockSpec(memory_space=pltpu.SMEM)


def dot(a, b, dims, precision):
    return lax.dot_general(a, b, (dims, ((), ())), precision=precision, preferred_element_type=F32)


def shift(value, axis, by):
    size = lax.axis_size(axis)
    return lax.ppermute(value, axis, [(i, (i + by) % size) for i in range(size)])


def exchange(value, axes):
    return lax.all_to_all(value, axes, 0, 0, tiled=True)


def spread(value, axes):
    return exchange(jnp.broadcast_to(value[None], (lax.axis_size(axes), *value.shape)), axes)


def split(value):
    high = value.astype(BF16)
    return high, (value - high.astype(F32)).astype(BF16)


def mul(a, b):
    f = lambda u, v: jnp.dot(u, v, preferred_element_type=F32)
    return f(a[0], b[0]) + (f(a[0], b[1]) + f(a[1], b[0]))


def band_rows(ref, lead, at, by, n_z):
    source = lax.rem(at + n_z - by, n_z)
    per = n_z // 2
    quarters = [ref[(*lead, per * lax.rem(source, 2) + i, source // 2)] for i in range(per)]
    return jnp.concatenate(quarters, axis=0)


def product_kernel(n_z, at_ref, matrix_ref, operand_ref, out_ref):
    width = matrix_ref.shape[1] // n_z
    slab = operand_ref.shape[-1]
    total = None
    for by in range(n_z):
        high, low = split(band_rows(operand_ref, (), at_ref[0], by, n_z))
        left = split(matrix_ref[:, by * width : (by + 1) * width])
        both = jnp.dot(left[0], jnp.concatenate([high, low], axis=1), preferred_element_type=F32)
        term = both[:, :slab] + (both[:, slab:] + jnp.dot(left[1], high, preferred_element_type=F32))
        total = term if total is None else total + term
    out_ref[...] = total.reshape(out_ref.shape)


def first_kernel(n_z, n_core, matrix_ref, operand_ref, out_ref):
    high, low = split(operand_ref[...])
    slab = operand_ref.shape[-1]
    left = split(matrix_ref[...])
    both = jnp.dot(left[0], jnp.concatenate([high, low], axis=1), preferred_element_type=F32)
    total = both[:, :slab] + (both[:, slab:] + jnp.dot(left[1], high, preferred_element_type=F32))
    quarter = out_ref.shape[-2]
    for k in range(n_core):
        for z in range(n_z):
            at = (k * n_z + z) * quarter
            out_ref[0, z, k] = total[at : at + quarter]


def apply_first(matrix, operand, n_y, n_z, n_core):
    rows, width = matrix.shape
    slab = operand.shape[1]
    quarter = rows // (n_y * n_z * n_core)
    return pl.pallas_call(
        functools.partial(first_kernel, n_z, n_core),
        grid=(n_y,),
        in_specs=[
            pl.BlockSpec((rows // n_y, width), lambda i: (i, 0)),
            pl.BlockSpec(operand.shape, lambda i: (0, 0)),
        ],
        out_specs=pl.BlockSpec((1, n_z, n_core, quarter, slab), lambda i: (i, 0, 0, 0, 0)),
        out_shape=jax.ShapeDtypeStruct((n_y, n_z, n_core, quarter, slab), F32),
        cost_estimate=pl.CostEstimate(
            flops=6 * rows * width * slab, bytes_accessed=4 * rows * width, transcendentals=0
        ),
    )(matrix, operand)


def apply_matrix(at_z, matrix, pieces, n_y):
    rows, band = matrix.shape
    slab = pieces.shape[-1]
    return pl.pallas_call(
        functools.partial(product_kernel, pieces.shape[0]),
        grid=(2,),
        in_specs=[
            SMEM,
            pl.BlockSpec((rows // 2, band), lambda i: (i, 0)),
            pl.BlockSpec(pieces.shape, lambda i: (0, 0, 0, 0)),
        ],
        out_specs=pl.BlockSpec((n_y // 2, rows // n_y, slab), lambda i: (i, 0, 0)),
        out_shape=jax.ShapeDtypeStruct((n_y, rows // n_y, slab), F32),
        cost_estimate=pl.CostEstimate(
            flops=6 * rows * band * slab, bytes_accessed=4 * rows * band, transcendentals=0
        ),
    )(at_z, matrix, pieces)


def trail_kernel(n_z, n_x, with_gram, one_list, at_ref, *refs):
    lists = refs[:1] if one_list else refs[:n_x]
    refs = refs[len(lists) :]
    factor = refs[: 2 * n_z]
    refs = refs[2 * n_z :]
    gram = refs[: 2 * n_z] if with_gram else ()
    start_ref, out_ref, high_ref, low_ref, chosen_ref = refs[len(gram) :]
    at_x, at_z = at_ref[0], at_ref[1]
    width = factor[0].shape[-1]
    slots = start_ref.shape[1] if with_gram else 0
    slab = out_ref.shape[-1]

    @pl.when(pl.program_id(0) == 0)
    def _():
        for by in range(n_z):
            for i in range(n_x):
                rows = band_rows(lists[0] if one_list else lists[i], (i,) if one_list else (), at_z, by, n_z)
                into = slice(by * width, (by + 1) * width), slice(i * slab, (i + 1) * slab)
                high_ref[into], low_ref[into] = split(rows)
            if with_gram:
                chosen_ref[by * slots : (by + 1) * slots, :] = start_ref[lax.rem(at_z + n_z - by, n_z)]

    def left(pieces):
        sides = [jnp.concatenate([v[0] for v in pieces[side * n_z :][:n_z]], axis=1) for side in range(2)]
        return split(jnp.concatenate(sides, axis=0))

    total = mul(left(factor), (high_ref[...], low_ref[...]))
    if with_gram:
        high, low = left(gram)
        chosen = chosen_ref[...]
        placed = jnp.dot(high, chosen, preferred_element_type=F32) + jnp.dot(low, chosen, preferred_element_type=F32)
        total = placed - total
    half = total.shape[0] // 2
    for i in range(n_x):
        at = i if one_list else lax.rem(at_x + i, n_x)
        for side in range(2):
            part = total[side * half : (side + 1) * half, i * slab : (i + 1) * slab]
            out_ref[at, side, 0] = part if with_gram else start_ref[at, side, 0] - part


def apply_trail(where, own, other, width, lists, start, with_gram, n_x):
    n_z = len(own)
    blocks, quarter, depth = own[0].shape
    slots = depth - width
    slab = lists[0].shape[-1]
    whole = lambda v: pl.BlockSpec(v.shape, lambda *_: (0,) * v.ndim)
    part = pl.BlockSpec((1, quarter, width), lambda t: (t, 0, 0))
    ends = pl.BlockSpec((n_x, 2, 1, quarter, slab), lambda t: (0, 0, t, 0, 0))
    pieces = [*own, *other]
    specs = [SMEM] + [whole(v) for v in lists] + [part] * (2 * n_z)
    args = [where, *lists, *pieces]
    if with_gram:
        specs += [pl.BlockSpec((1, quarter, slots), lambda t: (t, 0, width // slots))] * (2 * n_z)
        args += pieces
    band, n_list = n_z * width, n_x * slab
    return pl.pallas_call(
        functools.partial(trail_kernel, n_z, n_x, with_gram, len(lists) == 1),
        grid=(blocks,),
        in_specs=specs + [whole(start) if with_gram else ends],
        out_specs=ends,
        out_shape=jax.ShapeDtypeStruct((n_x, 2, blocks, quarter, slab), F32),
        scratch_shapes=[
            pltpu.VMEM((band, n_list), BF16),
            pltpu.VMEM((band, n_list), BF16),
            pltpu.VMEM((n_z * max(slots, 16), n_list), BF16),
        ],
        cost_estimate=pl.CostEstimate(
            flops=12 * blocks * quarter * band * n_list, bytes_accessed=10 * 2**20, transcendentals=0
        ),
    )(*args, start)


def rows_kernel(first_ref, second_ref, out_ref):
    n_y, wide = first_ref.shape[0], first_ref.shape[-1]
    for i in range(n_y):
        out_ref[0, :, i * wide : (i + 1) * wide] = first_ref[i, 0]
        out_ref[1, :, i * wide : (i + 1) * wide] = second_ref[i, 0]


def as_rows(first, second):
    n_y, n_z, quarter, wide = first.shape
    spec = pl.BlockSpec((n_y, 1, quarter, wide), lambda i: (0, i, 0, 0))
    return pl.pallas_call(
        rows_kernel,
        grid=(n_z,),
        in_specs=[spec, spec],
        out_specs=pl.BlockSpec((2, quarter, n_y * wide), lambda i: (0, i, 0)),
        out_shape=jax.ShapeDtypeStruct((2, n_z * quarter, n_y * wide), F32),
    )(first, second)


def after(value, *others):
    return lax.optimization_barrier((value, *others))[0]


def body(cells, gram_slots, diag_inverse, lower_block, trail_factor):
    n_x, n_core, n_y, n_z = (lax.axis_size(a) for a in ROWS + COLS)
    n_rows, n_cols = n_x * n_core, n_y * n_z
    col = lax.axis_index(COLS)
    row = lax.axis_index(ROWS)
    core = lax.axis_index("core")
    x_at = lax.axis_index("x")
    z_at = lax.axis_index("z")
    list_len = cells.shape[0]
    run_len = list_len // n_cols
    slab = list_len // n_rows
    runs_in_slab = slab // run_len
    block_rows = gram_slots.shape[1]
    capacity = gram_slots.shape[2]
    per_run = capacity // n_cols
    slab_slots = runs_in_slab * per_run
    width = diag_inverse.shape[2]
    trail_blocks = trail_factor.shape[0]
    quarter = block_rows // n_z
    sub = n_core * quarter

    owners = cells // (NCELL // n_cols)
    onehot = (owners[:, None] == jnp.arange(n_cols, dtype=jnp.int32)[None, :]).astype(jnp.int32)
    blocked = onehot.reshape(n_cols, run_len, n_cols)
    lower = jnp.tril(jnp.ones((run_len, run_len), F32), -1)
    in_run = jnp.einsum("ij,bjo->bio", lower, blocked.astype(F32)).astype(jnp.int32)
    run_total = jnp.sum(blocked, axis=1)
    runs = jnp.arange(n_cols)
    before = jnp.sum(jnp.where(runs[:, None, None] > runs[None, :, None], run_total[None, :, :], 0), axis=1)
    pair_rank = jnp.sum(in_run * blocked, axis=2).reshape(list_len)
    slots_of = pair_rank + jnp.sum(before[:, None, :] * blocked, axis=2).reshape(list_len)
    mine = owners == col
    position = jnp.arange(list_len, dtype=jnp.int32) // run_len * per_run + pair_rank
    slot_range = jnp.arange(capacity, dtype=jnp.int32)
    to_list = ((slots_of[None, :] == slot_range[:, None]) & mine[None, :]).astype(F32)
    to_runs = dot(
        ((position[None, :] == slot_range[:, None]) & mine[None, :]).astype(F32),
        to_list,
        ((1,), (1,)),
        lax.Precision.DEFAULT,
    )

    def moved(cut, by):
        return shift(cut((z_at + by) % n_z), "z", by) if by else cut(z_at)

    def quarters(cut):
        return [moved(cut, by) for by in range(n_z)]

    def rows_at(matrix, at):
        return lax.dynamic_slice_in_dim(matrix, at * quarter, quarter, matrix.ndim - 2)

    def all_rows(pieces):
        return lax.all_gather(jnp.concatenate(pieces, axis=1), ROWS, axis=0, tiled=True)

    inverse_0 = lax.all_gather(diag_inverse[0], ROWS, axis=0, tiled=True)

    outgoing = lax.dot_general(
        to_runs, gram_slots[0:2], (((1,), (2,)), ((), ())), precision=HIGHEST, preferred_element_type=F32
    )
    blocks = after(jnp.stack([lower_block, diag_inverse[1]]), outgoing)
    pieces = quarters(lambda at: rows_at(blocks, at))
    slab_gram = exchange(outgoing.reshape(n_rows, slab_slots, 2, block_rows), ROWS)
    pieces = list(lax.optimization_barrier((*pieces, slab_gram)))[:-1]
    below, inverse_1 = (all_rows([v[i] for v in pieces]) for i in range(2))
    by_width = slab_gram[:, :, 0].reshape(n_rows, slab_slots, block_rows // width, width)
    by_width = by_width.transpose(0, 2, 1, 3).reshape(n_cols, slab_slots, width)
    by_sub = slab_gram[:, :, 1].reshape(n_y, n_core, slab_slots, n_z, quarter).transpose(0, 3, 2, 1, 4)
    by_sub = by_sub.reshape(n_cols, slab_slots, sub)
    sub_gram = exchange(jnp.concatenate([by_width, by_sub], axis=2), COLS)
    slab_owner = lax.dynamic_slice_in_dim(owners, row * slab, slab)
    slab_rank = lax.dynamic_slice_in_dim(pair_rank, row * slab, slab)
    slab_slot = jnp.arange(slab, dtype=jnp.int32) // run_len * per_run + slab_rank
    from_owner = (
        jnp.arange(n_cols * slab_slots, dtype=jnp.int32)[:, None] == (slab_owner * slab_slots + slab_slot)[None, :]
    ).astype(F32)
    rhs = dot(sub_gram.reshape(n_cols * slab_slots, width + sub), from_owner, ((0,), (0,)), HIGHEST)

    where_z = z_at.astype(jnp.int32).reshape(1)

    def spread_z(block):
        return spread(block, "z").reshape(n_z, n_core, quarter, slab)

    def product(matrix, pieces):
        return jnp.sum(exchange(apply_matrix(where_z, matrix, pieces, n_y), "y"), axis=0)

    axes = ROWS + COLS
    sizes = (n_x, n_core, n_y, n_z)

    def device(x, k, y, z):
        return ((x * n_core + k) * n_y + y) * n_z + z

    def solution_rows(block):
        pieces = block.reshape(n_core, quarter, slab)
        moved = []
        for m in range(n_core):
            to = [
                (device(x, k, y, z), device(y, k ^ m, x, z))
                for x in range(n_x)
                for k in range(n_core)
                for y in range(n_y)
                for z in range(n_z)
            ]
            moved.append(lax.ppermute(lax.dynamic_index_in_dim(pieces, core ^ m, 0, keepdims=False), axes, to))
        piece = jnp.where(core == 0, jnp.concatenate(moved, axis=1), jnp.concatenate(moved[::-1], axis=1))
        return lax.all_gather(piece, COLS, axis=0, tiled=False)

    def trail_0(at):
        return jnp.concatenate([rows_at(early[0], at), rows_at(early[1], at)], axis=2)

    def trail_1(at):
        return rows_at(late, at)

    first = jnp.sum(
        exchange(apply_first(inverse_0, rhs[:width], n_y, n_z, n_core).reshape(n_cols, sub, slab), COLS), axis=0
    )
    first_pieces = spread_z(first)
    first_out = solution_rows(first)
    early = lax.optimization_barrier((trail_factor[:, 0], gram_slots[2:], first_pieces))
    own_0 = {by: moved(trail_0, by) for by in range(n_z) if by != n_z // 2}
    first_all = [first_pieces] + [shift(first_pieces, "x", -d) for d in range(1, n_x)]
    second_rhs = rhs[width:] - product(below, first_pieces)
    second_rhs = after(second_rhs, *own_0.values())
    second_pieces = spread_z(second_rhs)
    early = lax.optimization_barrier((trail_factor[:, 0], gram_slots[2:], second_pieces))
    late = after(trail_factor[:, 1], second_pieces)
    own_0[n_z // 2] = moved(trail_0, n_z // 2)
    own_0 = [own_0[by] for by in range(n_z)]
    own_1 = {by: moved(trail_1, by) for by in range(n_z) if by != n_z // 2}
    late = after(trail_factor[:, 1], outgoing)
    own_1[n_z // 2] = after(moved(trail_1, n_z // 2), slab_gram)
    own_1 = [own_1[by] for by in range(n_z)]
    other_0 = [shift(v, "core", 1) for v in own_0]
    other_1 = [shift(v, "core", 1) for v in own_1]

    trail_owner = col // n_z * n_z + jnp.arange(n_z, dtype=jnp.int32)
    slab_order = ((x_at + jnp.arange(n_x, dtype=jnp.int32)) % n_x * n_core + core)[:, None] * slab
    list_order = (slab_order + jnp.arange(slab, dtype=jnp.int32)[None, :]).reshape(-1)
    to_lists = (
        (jnp.take(slots_of, list_order)[None, None, :] == slot_range[None, :, None])
        & (jnp.take(owners, list_order)[None, None, :] == trail_owner[:, None, None])
    ).astype(BF16)
    where = jnp.stack([x_at, z_at]).astype(jnp.int32)
    base = apply_trail(where, own_0, other_0, width, first_all, to_lists, True, n_x)

    second = after(product(inverse_1, second_pieces), own_0[n_z // 2], *own_1, *first_all)
    second_out = solution_rows(second)
    second_all = spread(second, ("x", "z")).reshape(n_x, n_z, n_core, quarter, slab)
    terms = apply_trail(where, own_1, other_1, width, [second_all], base, False, n_x)
    total = jnp.sum(exchange(terms, "y"), axis=0).reshape(n_core, trail_blocks, quarter, slab)
    kept, given = total[0], total[1]
    got = shift(given, "core", 1)
    pair = jnp.where(core == 0, jnp.stack([kept, got]), jnp.stack([got, kept]))
    pair = pair.reshape(n_core, trail_blocks, quarter, n_z // n_core, run_len).transpose(0, 3, 1, 2, 4)
    out = exchange(pair.reshape(n_z, trail_blocks, quarter, run_len), "z")
    trail_out = out.transpose(1, 0, 2, 3).reshape(trail_blocks, block_rows, run_len)
    return as_rows(*(v.reshape(n_y, n_z, quarter, n_core * slab) for v in (first_out, second_out))), trail_out


def solution(mesh):
    n_rows, n_cols = mesh.devices.shape
    side = int(round(n_cols**0.5))
    mesh = Mesh(mesh.devices.reshape(n_rows // 2, 2, side, n_cols // side), ROWS + COLS)
    return jax.shard_map(
        body,
        mesh=mesh,
        in_specs=(
            P(),
            P(None, ROWS, COLS),
            P(None, ROWS, COLS),
            P(ROWS, COLS),
            P(None, None, ROWS, COLS),
        ),
        out_specs=(P(None, ROWS, None), P(None, ROWS, COLS)),
        check_vma=False,
    )
```

```python
import functools

import jax
import jax.numpy as jnp
from jax import lax
from jax.experimental import pallas as pl
from jax.experimental.pallas import tpu as pltpu
from jax.sharding import Mesh
from jax.sharding import PartitionSpec as P

NCELL = 65536
ROWS = ("x", "core")
COLS = ("y", "z")
HIGHEST = lax.Precision.HIGHEST
F32 = jnp.float32
BF16 = jnp.bfloat16
SMEM = pl.BlockSpec(memory_space=pltpu.SMEM)


def dot(a, b, dims, precision):
    return lax.dot_general(a, b, (dims, ((), ())), precision=precision, preferred_element_type=F32)


def shift(value, axis, by):
    size = lax.axis_size(axis)
    return lax.ppermute(value, axis, [(i, (i + by) % size) for i in range(size)])


def exchange(value, axes):
    return lax.all_to_all(value, axes, 0, 0, tiled=True)


def spread(value, axes):
    return exchange(jnp.broadcast_to(value[None], (lax.axis_size(axes), *value.shape)), axes)


def split(value):
    high = value.astype(BF16)
    return high, (value - high.astype(F32)).astype(BF16)


def mul(a, b):
    f = lambda u, v: jnp.dot(u, v, preferred_element_type=F32)
    return f(a[0], b[0]) + (f(a[0], b[1]) + f(a[1], b[0]))


def band_rows(ref, lead, at, by, n_z):
    source = lax.rem(at + n_z - by, n_z)
    per = n_z // 2
    quarters = [ref[(*lead, per * lax.rem(source, 2) + i, source // 2)] for i in range(per)]
    return jnp.concatenate(quarters, axis=0)


def product_kernel(n_z, at_ref, matrix_ref, operand_ref, out_ref):
    width = matrix_ref.shape[1] // n_z
    slab = operand_ref.shape[-1]
    total = None
    for by in range(n_z):
        high, low = split(band_rows(operand_ref, (), at_ref[0], by, n_z))
        left = split(matrix_ref[:, by * width : (by + 1) * width])
        both = jnp.dot(left[0], jnp.concatenate([high, low], axis=1), preferred_element_type=F32)
        term = both[:, :slab] + (both[:, slab:] + jnp.dot(left[1], high, preferred_element_type=F32))
        total = term if total is None else total + term
    out_ref[...] = total.reshape(out_ref.shape)


def first_kernel(n_z, n_core, matrix_ref, operand_ref, out_ref):
    high, low = split(operand_ref[...])
    slab = operand_ref.shape[-1]
    left = split(matrix_ref[...])
    both = jnp.dot(left[0], jnp.concatenate([high, low], axis=1), preferred_element_type=F32)
    total = both[:, :slab] + (both[:, slab:] + jnp.dot(left[1], high, preferred_element_type=F32))
    quarter = out_ref.shape[-2]
    for k in range(n_core):
        for z in range(n_z):
            at = (k * n_z + z) * quarter
            out_ref[0, z, k] = total[at : at + quarter]


def apply_first(matrix, operand, n_y, n_z, n_core):
    rows, width = matrix.shape
    slab = operand.shape[1]
    quarter = rows // (n_y * n_z * n_core)
    return pl.pallas_call(
        functools.partial(first_kernel, n_z, n_core),
        grid=(n_y,),
        in_specs=[
            pl.BlockSpec((rows // n_y, width), lambda i: (i, 0)),
            pl.BlockSpec(operand.shape, lambda i: (0, 0)),
        ],
        out_specs=pl.BlockSpec((1, n_z, n_core, quarter, slab), lambda i: (i, 0, 0, 0, 0)),
        out_shape=jax.ShapeDtypeStruct((n_y, n_z, n_core, quarter, slab), F32),
        cost_estimate=pl.CostEstimate(
            flops=6 * rows * width * slab, bytes_accessed=4 * rows * width, transcendentals=0
        ),
    )(matrix, operand)


def apply_matrix(at_z, matrix, pieces, n_y):
    rows, band = matrix.shape
    slab = pieces.shape[-1]
    return pl.pallas_call(
        functools.partial(product_kernel, pieces.shape[0]),
        grid=(2,),
        in_specs=[
            SMEM,
            pl.BlockSpec((rows // 2, band), lambda i: (i, 0)),
            pl.BlockSpec(pieces.shape, lambda i: (0, 0, 0, 0)),
        ],
        out_specs=pl.BlockSpec((n_y // 2, rows // n_y, slab), lambda i: (i, 0, 0)),
        out_shape=jax.ShapeDtypeStruct((n_y, rows // n_y, slab), F32),
        cost_estimate=pl.CostEstimate(
            flops=6 * rows * band * slab, bytes_accessed=4 * rows * band, transcendentals=0
        ),
    )(at_z, matrix, pieces)


def trail_kernel(n_z, with_gram, at_ref, lists_ref, *refs):
    factor = refs[: 2 * n_z]
    refs = refs[2 * n_z :]
    gram = refs[: 2 * n_z] if with_gram else ()
    start_ref, out_ref, high_ref, low_ref, chosen_ref = refs[len(gram) :]
    n_x, at_z = lists_ref.shape[0], at_ref[0]
    width = factor[0].shape[-1]
    slots = start_ref.shape[1] if with_gram else 0
    slab = out_ref.shape[-1]

    @pl.when(pl.program_id(0) == 0)
    def _():
        for by in range(n_z):
            for i in range(n_x):
                rows = band_rows(lists_ref, (i,), at_z, by, n_z)
                into = slice(by * width, (by + 1) * width), slice(i * slab, (i + 1) * slab)
                high_ref[into], low_ref[into] = split(rows)
            if with_gram:
                chosen_ref[by * slots : (by + 1) * slots, :] = start_ref[lax.rem(at_z + n_z - by, n_z)]

    def left(pieces):
        sides = [jnp.concatenate([v[0] for v in pieces[side * n_z :][:n_z]], axis=1) for side in range(2)]
        return split(jnp.concatenate(sides, axis=0))

    total = mul(left(factor), (high_ref[...], low_ref[...]))
    if with_gram:
        high, low = left(gram)
        chosen = chosen_ref[...]
        placed = jnp.dot(high, chosen, preferred_element_type=F32) + jnp.dot(low, chosen, preferred_element_type=F32)
        total = placed - total
    half = total.shape[0] // 2
    for i in range(n_x):
        for side in range(2):
            part = total[side * half : (side + 1) * half, i * slab : (i + 1) * slab]
            out_ref[i, side, 0] = part if with_gram else start_ref[i, side, 0] - part


def apply_trail(where, own, other, width, lists, start, with_gram):
    n_z = len(own)
    blocks, quarter, depth = own[0].shape
    slots = depth - width
    n_x, slab = lists.shape[0], lists.shape[-1]
    whole = lambda v: pl.BlockSpec(v.shape, lambda *_: (0,) * v.ndim)
    part = pl.BlockSpec((1, quarter, width), lambda t: (t, 0, 0))
    ends = pl.BlockSpec((n_x, 2, 1, quarter, slab), lambda t: (0, 0, t, 0, 0))
    pieces = [*own, *other]
    specs = [SMEM, whole(lists)] + [part] * (2 * n_z)
    args = [where, lists, *pieces]
    if with_gram:
        specs += [pl.BlockSpec((1, quarter, slots), lambda t: (t, 0, width // slots))] * (2 * n_z)
        args += pieces
    band, n_list = n_z * width, n_x * slab
    return pl.pallas_call(
        functools.partial(trail_kernel, n_z, with_gram),
        grid=(blocks,),
        in_specs=specs + [whole(start) if with_gram else ends],
        out_specs=ends,
        out_shape=jax.ShapeDtypeStruct((n_x, 2, blocks, quarter, slab), F32),
        scratch_shapes=[
            pltpu.VMEM((band, n_list), BF16),
            pltpu.VMEM((band, n_list), BF16),
            pltpu.VMEM((n_z * max(slots, 16), n_list), BF16),
        ],
        cost_estimate=pl.CostEstimate(
            flops=12 * blocks * quarter * band * n_list, bytes_accessed=10 * 2**20, transcendentals=0
        ),
    )(*args, start)


def rows_kernel(at_ref, first_ref, *refs):
    seconds, out_ref = refs[:-1], refs[-1]
    n_y, n_z, quarter, wide = first_ref.shape
    for y in range(n_y):
        at_y = pl.multiple_of(lax.rem(at_ref[0] + n_y - y, n_y) * wide, wide)
        for z in range(n_z):
            out_ref[0, z * quarter : (z + 1) * quarter, y * wide : (y + 1) * wide] = first_ref[y, z]
            at_z = pl.multiple_of(lax.rem(at_ref[1] + n_z - z, n_z) * quarter, quarter)
            out_ref[1, pl.ds(at_z, quarter), pl.ds(at_y, wide)] = seconds[y][z]


def as_rows(where, first, seconds):
    n_y, n_z, quarter, wide = first.shape
    return pl.pallas_call(
        rows_kernel,
        in_specs=[SMEM] + [pl.BlockSpec(memory_space=pltpu.VMEM)] * (1 + n_y),
        out_specs=pl.BlockSpec(memory_space=pltpu.VMEM),
        out_shape=jax.ShapeDtypeStruct((2, n_z * quarter, n_y * wide), F32),
        cost_estimate=pl.CostEstimate(flops=0, bytes_accessed=8 * 2**20, transcendentals=0),
    )(where, first, *seconds)


def after(value, *others):
    return lax.optimization_barrier((value, *others))[0]


def body(cells, gram_slots, diag_inverse, lower_block, trail_factor):
    n_x, n_core, n_y, n_z = (lax.axis_size(a) for a in ROWS + COLS)
    n_rows, n_cols = n_x * n_core, n_y * n_z
    col = lax.axis_index(COLS)
    row = lax.axis_index(ROWS)
    core = lax.axis_index("core")
    y_at = lax.axis_index("y")
    z_at = lax.axis_index("z")
    list_len = cells.shape[0]
    run_len = list_len // n_cols
    slab = list_len // n_rows
    runs_in_slab = slab // run_len
    block_rows = gram_slots.shape[1]
    capacity = gram_slots.shape[2]
    per_run = capacity // n_cols
    slab_slots = runs_in_slab * per_run
    width = diag_inverse.shape[2]
    trail_blocks = trail_factor.shape[0]
    quarter = block_rows // n_z
    sub = n_core * quarter

    owners = cells // (NCELL // n_cols)
    onehot = (owners[:, None] == jnp.arange(n_cols, dtype=jnp.int32)[None, :]).astype(jnp.int32)
    blocked = onehot.reshape(n_cols, run_len, n_cols)
    lower = jnp.tril(jnp.ones((run_len, run_len), F32), -1)
    in_run = jnp.einsum("ij,bjo->bio", lower, blocked.astype(F32)).astype(jnp.int32)
    run_total = jnp.sum(blocked, axis=1)
    runs = jnp.arange(n_cols)
    before = jnp.sum(jnp.where(runs[:, None, None] > runs[None, :, None], run_total[None, :, :], 0), axis=1)
    pair_rank = jnp.sum(in_run * blocked, axis=2).reshape(list_len)
    slots_of = pair_rank + jnp.sum(before[:, None, :] * blocked, axis=2).reshape(list_len)
    mine = owners == col
    position = jnp.arange(list_len, dtype=jnp.int32) // run_len * per_run + pair_rank
    slot_range = jnp.arange(capacity, dtype=jnp.int32)
    to_list = ((slots_of[None, :] == slot_range[:, None]) & mine[None, :]).astype(F32)
    to_runs = dot(
        ((position[None, :] == slot_range[:, None]) & mine[None, :]).astype(F32),
        to_list,
        ((1,), (1,)),
        lax.Precision.DEFAULT,
    )

    def moved(cut, by, ready=None):
        value = cut((z_at + by) % n_z)
        return shift(value if ready is None else after(value, ready), "z", by) if by else value

    def quarters(cut):
        return [moved(cut, by) for by in range(n_z)]

    def rows_at(matrix, at):
        return lax.dynamic_slice_in_dim(matrix, at * quarter, quarter, matrix.ndim - 2)

    def all_rows(pieces):
        return lax.all_gather(jnp.concatenate(pieces, axis=1), ROWS, axis=0, tiled=True)

    inverse_0 = lax.all_gather(diag_inverse[0], ROWS, axis=0, tiled=True)

    outgoing = lax.dot_general(
        to_runs, gram_slots[0:2], (((1,), (2,)), ((), ())), precision=HIGHEST, preferred_element_type=F32
    )
    blocks = after(jnp.stack([lower_block, diag_inverse[1]]), outgoing)
    pieces = quarters(lambda at: rows_at(blocks, at))
    slab_gram = exchange(outgoing.reshape(n_rows, slab_slots, 2, block_rows), ROWS)
    pieces = list(lax.optimization_barrier((*pieces, slab_gram)))[:-1]
    below, inverse_1 = (all_rows([v[i] for v in pieces]) for i in range(2))
    by_width = slab_gram[:, :, 0].reshape(n_rows, slab_slots, block_rows // width, width)
    by_width = by_width.transpose(0, 2, 1, 3).reshape(n_cols, slab_slots, width)
    by_sub = slab_gram[:, :, 1].reshape(n_y, n_core, slab_slots, n_z, quarter).transpose(0, 3, 2, 1, 4)
    by_sub = by_sub.reshape(n_cols, slab_slots, sub)
    sub_gram = exchange(jnp.concatenate([by_width, by_sub], axis=2), COLS)
    slab_owner = lax.dynamic_slice_in_dim(owners, row * slab, slab)
    slab_rank = lax.dynamic_slice_in_dim(pair_rank, row * slab, slab)
    slab_slot = jnp.arange(slab, dtype=jnp.int32) // run_len * per_run + slab_rank
    from_owner = (
        jnp.arange(n_cols * slab_slots, dtype=jnp.int32)[:, None] == (slab_owner * slab_slots + slab_slot)[None, :]
    ).astype(F32)
    rhs = dot(sub_gram.reshape(n_cols * slab_slots, width + sub), from_owner, ((0,), (0,)), HIGHEST)

    where_z = z_at.astype(jnp.int32).reshape(1)

    def spread_z(block):
        return spread(block, "z").reshape(n_z, n_core, quarter, slab)

    def summed(terms, axes):
        return jnp.sum(exchange(terms, axes), axis=0)

    axes = ROWS + COLS
    sizes = (n_x, n_core, n_y, n_z)

    def device(x, k, y, z):
        return ((x * n_core + k) * n_y + y) * n_z + z

    def solution_piece(block):
        pieces = block.reshape(n_core, quarter, slab)
        arrived = []
        for m in range(n_core):
            to = [
                (device(x, k, y, z), device(y, k ^ m, x, z))
                for x in range(n_x)
                for k in range(n_core)
                for y in range(n_y)
                for z in range(n_z)
            ]
            arrived.append(lax.ppermute(lax.dynamic_index_in_dim(pieces, core ^ m, 0, keepdims=False), axes, to))
        return jnp.where(core == 0, jnp.concatenate(arrived, axis=1), jnp.concatenate(arrived[::-1], axis=1))

    def trail_0(at):
        return jnp.concatenate([rows_at(trail_factor[:, 0], at), rows_at(gram_slots[2:], at)], axis=2)

    def trail_1(at):
        return rows_at(trail_factor[:, 1], at)

    far = n_z // 2
    near = [by for by in range(1, n_z) if by != far]
    own_0, own_1 = {0: trail_0(z_at)}, {0: trail_1(z_at)}
    terms = apply_first(inverse_0, rhs[:width], n_y, n_z, n_core)
    own_1[far] = moved(trail_1, far, slab_gram)
    own_1.update({by: moved(trail_1, by, terms) for by in near})
    first = after(summed(terms.reshape(n_cols, sub, slab), COLS), *own_1.values())
    first_pieces = spread_z(first)
    first_all = lax.all_gather(first_pieces, "x", axis=0, tiled=False)
    first_piece = solution_piece(first)
    first_out = lax.all_gather(first_piece, COLS, axis=0, tiled=False)

    terms = apply_matrix(where_z, below, first_pieces, n_y)
    own_0.update({by: moved(trail_0, by, terms) for by in near})
    second_rhs = after(rhs[width:] - summed(terms, "y"), first_piece, *own_0.values())
    second_pieces = spread_z(second_rhs)

    terms = apply_matrix(where_z, inverse_1, second_pieces, n_y)
    own_0[far] = moved(trail_0, far, terms)
    own_0, own_1 = ([own[by] for by in range(n_z)] for own in (own_0, own_1))
    other_0 = [shift(v, "core", 1) for v in own_0]
    other_1 = [shift(v, "core", 1) for v in own_1]

    trail_owner = col // n_z * n_z + jnp.arange(n_z, dtype=jnp.int32)
    slab_order = (jnp.arange(n_x, dtype=jnp.int32) * n_core + core)[:, None] * slab
    list_order = (slab_order + jnp.arange(slab, dtype=jnp.int32)[None, :]).reshape(-1)
    to_lists = (
        (jnp.take(slots_of, list_order)[None, None, :] == slot_range[None, :, None])
        & (jnp.take(owners, list_order)[None, None, :] == trail_owner[:, None, None])
    ).astype(BF16)
    base = apply_trail(where_z, own_0, other_0, width, first_all, to_lists, True)

    second = after(summed(terms, "y"), own_0[far])
    piece = solution_piece(second)
    piece = jnp.stack([piece] + [shift(piece, "z", by) for by in range(1, n_z)])
    second_out = [piece] + [shift(piece, "y", by) for by in range(1, n_y)]
    second_all = spread(second, ("x", "z")).reshape(n_x, n_z, n_core, quarter, slab)
    terms = apply_trail(where_z, own_1, other_1, width, second_all, base, False)
    terms = after(terms, *second_out)
    total = summed(terms, "y").reshape(n_core, trail_blocks, quarter, slab)
    kept, given = total[0], total[1]
    got = shift(given, "core", 1)
    pair = jnp.where(core == 0, jnp.stack([kept, got]), jnp.stack([got, kept]))
    pair = pair.reshape(n_core, trail_blocks, quarter, n_z // n_core, run_len).transpose(0, 3, 1, 2, 4)
    out = exchange(pair.reshape(n_z, trail_blocks, quarter, run_len), "z")
    trail_out = out.transpose(1, 0, 2, 3).reshape(trail_blocks, block_rows, run_len)
    first_out = first_out.reshape(n_y, n_z, quarter, n_core * slab)
    return as_rows(jnp.stack([y_at, z_at]).astype(jnp.int32), first_out, second_out), trail_out


def solution(mesh):
    n_rows, n_cols = mesh.devices.shape
    side = int(round(n_cols**0.5))
    mesh = Mesh(mesh.devices.reshape(n_rows // 2, 2, side, n_cols // side), ROWS + COLS)
    return jax.shard_map(
        body,
        mesh=mesh,
        in_specs=(
            P(),
            P(None, ROWS, COLS),
            P(None, ROWS, COLS),
            P(ROWS, COLS),
            P(None, None, ROWS, COLS),
        ),
        out_specs=(P(None, ROWS, None), P(None, ROWS, COLS)),
        check_vma=False,
    )
```

```python
import functools

import jax
import jax.numpy as jnp
from jax import lax
from jax.experimental import pallas as pl
from jax.experimental.pallas import tpu as pltpu
from jax.sharding import Mesh
from jax.sharding import PartitionSpec as P

NCELL = 65536
ROWS = ("x", "core")
COLS = ("y", "z")
HIGHEST = lax.Precision.HIGHEST
F32 = jnp.float32
BF16 = jnp.bfloat16
SMEM = pl.BlockSpec(memory_space=pltpu.SMEM)


def dot(a, b, dims, precision):
    return lax.dot_general(a, b, (dims, ((), ())), precision=precision, preferred_element_type=F32)


def shift(value, axis, by):
    size = lax.axis_size(axis)
    return lax.ppermute(value, axis, [(i, (i + by) % size) for i in range(size)])


def exchange(value, axes):
    return lax.all_to_all(value, axes, 0, 0, tiled=True)


def spread(value, axes):
    return exchange(jnp.broadcast_to(value[None], (lax.axis_size(axes), *value.shape)), axes)


def split(value):
    high = value.astype(BF16)
    return high, (value - high.astype(F32)).astype(BF16)


def mul(a, b):
    f = lambda u, v: jnp.dot(u, v, preferred_element_type=F32)
    return f(a[0], b[0]) + (f(a[0], b[1]) + f(a[1], b[0]))


def band_rows(ref, lead, at, by, n_z):
    source = lax.rem(at + n_z - by, n_z)
    per = n_z // 2
    quarters = [ref[(*lead, per * lax.rem(source, 2) + i, source // 2)] for i in range(per)]
    return jnp.concatenate(quarters, axis=0)


def product_kernel(n_z, at_ref, matrix_ref, operand_ref, out_ref):
    width = matrix_ref.shape[1] // n_z
    slab = operand_ref.shape[-1]
    total = None
    for by in range(n_z):
        high, low = split(band_rows(operand_ref, (), at_ref[0], by, n_z))
        left = split(matrix_ref[:, by * width : (by + 1) * width])
        both = jnp.dot(left[0], jnp.concatenate([high, low], axis=1), preferred_element_type=F32)
        term = both[:, :slab] + (both[:, slab:] + jnp.dot(left[1], high, preferred_element_type=F32))
        total = term if total is None else total + term
    out_ref[...] = total.reshape(out_ref.shape)


def first_kernel(n_z, n_core, matrix_ref, operand_ref, out_ref):
    high, low = split(operand_ref[...])
    slab = operand_ref.shape[-1]
    left = split(matrix_ref[...])
    both = jnp.dot(left[0], jnp.concatenate([high, low], axis=1), preferred_element_type=F32)
    total = both[:, :slab] + (both[:, slab:] + jnp.dot(left[1], high, preferred_element_type=F32))
    quarter = out_ref.shape[-2]
    for k in range(n_core):
        for z in range(n_z):
            at = (k * n_z + z) * quarter
            out_ref[0, z, k] = total[at : at + quarter]


def apply_first(matrix, operand, n_y, n_z, n_core):
    rows, width = matrix.shape
    slab = operand.shape[1]
    quarter = rows // (n_y * n_z * n_core)
    return pl.pallas_call(
        functools.partial(first_kernel, n_z, n_core),
        grid=(n_y,),
        in_specs=[
            pl.BlockSpec((rows // n_y, width), lambda i: (i, 0)),
            pl.BlockSpec(operand.shape, lambda i: (0, 0)),
        ],
        out_specs=pl.BlockSpec((1, n_z, n_core, quarter, slab), lambda i: (i, 0, 0, 0, 0)),
        out_shape=jax.ShapeDtypeStruct((n_y, n_z, n_core, quarter, slab), F32),
        cost_estimate=pl.CostEstimate(
            flops=6 * rows * width * slab, bytes_accessed=4 * rows * width, transcendentals=0
        ),
    )(matrix, operand)


def apply_matrix(at_z, matrix, pieces, n_y):
    rows, band = matrix.shape
    slab = pieces.shape[-1]
    return pl.pallas_call(
        functools.partial(product_kernel, pieces.shape[0]),
        grid=(2,),
        in_specs=[
            SMEM,
            pl.BlockSpec((rows // 2, band), lambda i: (i, 0)),
            pl.BlockSpec(pieces.shape, lambda i: (0, 0, 0, 0)),
        ],
        out_specs=pl.BlockSpec((n_y // 2, rows // n_y, slab), lambda i: (i, 0, 0)),
        out_shape=jax.ShapeDtypeStruct((n_y, rows // n_y, slab), F32),
        cost_estimate=pl.CostEstimate(
            flops=6 * rows * band * slab, bytes_accessed=4 * rows * band, transcendentals=0
        ),
    )(at_z, matrix, pieces)


def trail_kernel(n_z, with_gram, at_ref, lists_ref, *refs):
    factor = refs[: 2 * n_z]
    refs = refs[2 * n_z :]
    gram = refs[: 2 * n_z] if with_gram else ()
    start_ref, out_ref, high_ref, low_ref, chosen_ref = refs[len(gram) :]
    n_x, at_z = lists_ref.shape[0], at_ref[0]
    width = factor[0].shape[-1]
    slots = start_ref.shape[1] if with_gram else 0
    slab = out_ref.shape[-1]

    @pl.when(pl.program_id(0) == 0)
    def _():
        for by in range(n_z):
            for i in range(n_x):
                rows = band_rows(lists_ref, (i,), at_z, by, n_z)
                into = slice(by * width, (by + 1) * width), slice(i * slab, (i + 1) * slab)
                high_ref[into], low_ref[into] = split(rows)
            if with_gram:
                chosen_ref[by * slots : (by + 1) * slots, :] = start_ref[lax.rem(at_z + n_z - by, n_z)]

    def left(pieces):
        sides = [jnp.concatenate([v[0] for v in pieces[side * n_z :][:n_z]], axis=1) for side in range(2)]
        return split(jnp.concatenate(sides, axis=0))

    total = mul(left(factor), (high_ref[...], low_ref[...]))
    if with_gram:
        high, low = left(gram)
        chosen = chosen_ref[...]
        placed = jnp.dot(high, chosen, preferred_element_type=F32) + jnp.dot(low, chosen, preferred_element_type=F32)
        total = placed - total
    half = total.shape[0] // 2
    for i in range(n_x):
        for side in range(2):
            part = total[side * half : (side + 1) * half, i * slab : (i + 1) * slab]
            out_ref[i, side, 0] = part if with_gram else start_ref[i, side, 0] - part


def apply_trail(where, own, other, width, lists, start, with_gram):
    n_z = len(own)
    blocks, quarter, depth = own[0].shape
    slots = depth - width
    n_x, slab = lists.shape[0], lists.shape[-1]
    whole = lambda v: pl.BlockSpec(v.shape, lambda *_: (0,) * v.ndim)
    part = pl.BlockSpec((1, quarter, width), lambda t: (t, 0, 0))
    ends = pl.BlockSpec((n_x, 2, 1, quarter, slab), lambda t: (0, 0, t, 0, 0))
    pieces = [*own, *other]
    specs = [SMEM, whole(lists)] + [part] * (2 * n_z)
    args = [where, lists, *pieces]
    if with_gram:
        specs += [pl.BlockSpec((1, quarter, slots), lambda t: (t, 0, width // slots))] * (2 * n_z)
        args += pieces
    band, n_list = n_z * width, n_x * slab
    return pl.pallas_call(
        functools.partial(trail_kernel, n_z, with_gram),
        grid=(blocks,),
        in_specs=specs + [whole(start) if with_gram else ends],
        out_specs=ends,
        out_shape=jax.ShapeDtypeStruct((n_x, 2, blocks, quarter, slab), F32),
        scratch_shapes=[
            pltpu.VMEM((band, n_list), BF16),
            pltpu.VMEM((band, n_list), BF16),
            pltpu.VMEM((n_z * max(slots, 16), n_list), BF16),
        ],
        cost_estimate=pl.CostEstimate(
            flops=12 * blocks * quarter * band * n_list, bytes_accessed=10 * 2**20, transcendentals=0
        ),
    )(*args, start)


def rows_kernel(at_ref, first_ref, *refs):
    seconds, out_ref = refs[:-1], refs[-1]
    n_y, n_z, quarter, wide = first_ref.shape
    for y in range(n_y):
        at_y = pl.multiple_of(lax.rem(at_ref[0] + n_y - y, n_y) * wide, wide)
        for z in range(n_z):
            out_ref[0, z * quarter : (z + 1) * quarter, y * wide : (y + 1) * wide] = first_ref[y, z]
            at_z = pl.multiple_of(lax.rem(at_ref[1] + n_z - z, n_z) * quarter, quarter)
            out_ref[1, pl.ds(at_z, quarter), pl.ds(at_y, wide)] = seconds[y][z]


def as_rows(where, first, seconds):
    n_y, n_z, quarter, wide = first.shape
    return pl.pallas_call(
        rows_kernel,
        in_specs=[SMEM] + [pl.BlockSpec(memory_space=pltpu.VMEM)] * (1 + n_y),
        out_specs=pl.BlockSpec(memory_space=pltpu.VMEM),
        out_shape=jax.ShapeDtypeStruct((2, n_z * quarter, n_y * wide), F32),
        cost_estimate=pl.CostEstimate(flops=0, bytes_accessed=8 * 2**20, transcendentals=0),
    )(where, first, *seconds)


def after(value, *others):
    return lax.optimization_barrier((value, *others))[0]


def body(cells, gram_slots, diag_inverse, lower_block, trail_factor):
    n_x, n_core, n_y, n_z = (lax.axis_size(a) for a in ROWS + COLS)
    n_rows, n_cols = n_x * n_core, n_y * n_z
    col = lax.axis_index(COLS)
    row = lax.axis_index(ROWS)
    core = lax.axis_index("core")
    y_at = lax.axis_index("y")
    z_at = lax.axis_index("z")
    list_len = cells.shape[0]
    run_len = list_len // n_cols
    slab = list_len // n_rows
    runs_in_slab = slab // run_len
    block_rows = gram_slots.shape[1]
    capacity = gram_slots.shape[2]
    per_run = capacity // n_cols
    slab_slots = runs_in_slab * per_run
    width = diag_inverse.shape[2]
    trail_blocks = trail_factor.shape[0]
    quarter = block_rows // n_z
    sub = n_core * quarter

    owners = cells // (NCELL // n_cols)
    onehot = (owners[:, None] == jnp.arange(n_cols, dtype=jnp.int32)[None, :]).astype(jnp.int32)
    blocked = onehot.reshape(n_cols, run_len, n_cols)
    lower = jnp.tril(jnp.ones((run_len, run_len), F32), -1)
    in_run = jnp.einsum("ij,bjo->bio", lower, blocked.astype(F32)).astype(jnp.int32)
    run_total = jnp.sum(blocked, axis=1)
    runs = jnp.arange(n_cols)
    before = jnp.sum(jnp.where(runs[:, None, None] > runs[None, :, None], run_total[None, :, :], 0), axis=1)
    pair_rank = jnp.sum(in_run * blocked, axis=2).reshape(list_len)
    slots_of = pair_rank + jnp.sum(before[:, None, :] * blocked, axis=2).reshape(list_len)
    mine = owners == col
    position = jnp.arange(list_len, dtype=jnp.int32) // run_len * per_run + pair_rank
    slot_range = jnp.arange(capacity, dtype=jnp.int32)
    to_list = ((slots_of[None, :] == slot_range[:, None]) & mine[None, :]).astype(F32)
    to_runs = dot(
        ((position[None, :] == slot_range[:, None]) & mine[None, :]).astype(F32),
        to_list,
        ((1,), (1,)),
        lax.Precision.DEFAULT,
    )

    def moved(cut, by, ready=None):
        value = cut((z_at + by) % n_z)
        return shift(value if ready is None else after(value, ready), "z", by) if by else value

    def quarters(cut):
        return [moved(cut, by) for by in range(n_z)]

    def rows_at(matrix, at):
        return lax.dynamic_slice_in_dim(matrix, at * quarter, quarter, matrix.ndim - 2)

    def all_rows(pieces):
        return lax.all_gather(jnp.concatenate(pieces, axis=1), ROWS, axis=0, tiled=True)

    inverse_0 = lax.all_gather(diag_inverse[0], ROWS, axis=0, tiled=True)

    outgoing = lax.dot_general(
        to_runs, gram_slots[0:2], (((1,), (2,)), ((), ())), precision=HIGHEST, preferred_element_type=F32
    )
    blocks = after(jnp.stack([lower_block, diag_inverse[1]]), outgoing)
    pieces = quarters(lambda at: rows_at(blocks, at))
    slab_gram = exchange(outgoing.reshape(n_rows, slab_slots, 2, block_rows), ROWS)
    pieces = list(lax.optimization_barrier((*pieces, slab_gram)))[:-1]
    below, inverse_1 = (all_rows([v[i] for v in pieces]) for i in range(2))
    by_width = slab_gram[:, :, 0].reshape(n_rows, slab_slots, block_rows // width, width)
    by_width = by_width.transpose(0, 2, 1, 3).reshape(n_cols, slab_slots, width)
    by_sub = slab_gram[:, :, 1].reshape(n_y, n_core, slab_slots, n_z, quarter).transpose(0, 3, 2, 1, 4)
    by_sub = by_sub.reshape(n_cols, slab_slots, sub)
    sub_gram = exchange(jnp.concatenate([by_width, by_sub], axis=2), COLS)
    slab_owner = lax.dynamic_slice_in_dim(owners, row * slab, slab)
    slab_rank = lax.dynamic_slice_in_dim(pair_rank, row * slab, slab)
    slab_slot = jnp.arange(slab, dtype=jnp.int32) // run_len * per_run + slab_rank
    from_owner = (
        jnp.arange(n_cols * slab_slots, dtype=jnp.int32)[:, None] == (slab_owner * slab_slots + slab_slot)[None, :]
    ).astype(F32)
    rhs = dot(sub_gram.reshape(n_cols * slab_slots, width + sub), from_owner, ((0,), (0,)), HIGHEST)

    where_z = z_at.astype(jnp.int32).reshape(1)

    def spread_z(block):
        return spread(block, "z").reshape(n_z, n_core, quarter, slab)

    def summed(terms, axes):
        return jnp.sum(exchange(terms, axes), axis=0)

    axes = ROWS + COLS
    sizes = (n_x, n_core, n_y, n_z)

    def device(x, k, y, z):
        return ((x * n_core + k) * n_y + y) * n_z + z

    def solution_piece(block):
        pieces = block.reshape(n_core, quarter, slab)
        arrived = []
        for m in range(n_core):
            to = [
                (device(x, k, y, z), device(y, k ^ m, x, z))
                for x in range(n_x)
                for k in range(n_core)
                for y in range(n_y)
                for z in range(n_z)
            ]
            arrived.append(lax.ppermute(lax.dynamic_index_in_dim(pieces, core ^ m, 0, keepdims=False), axes, to))
        return jnp.where(core == 0, jnp.concatenate(arrived, axis=1), jnp.concatenate(arrived[::-1], axis=1))

    def trail_0(at):
        return jnp.concatenate([rows_at(trail_factor[:, 0], at), rows_at(gram_slots[2:], at)], axis=2)

    def trail_1(at):
        return rows_at(trail_factor[:, 1], at)

    far = n_z // 2
    near = [by for by in range(1, n_z) if by != far]
    own_0, own_1 = {0: trail_0(z_at)}, {0: trail_1(z_at)}
    terms = apply_first(inverse_0, rhs[:width], n_y, n_z, n_core)
    own_1[far] = moved(trail_1, far, slab_gram)
    own_1.update({by: moved(trail_1, by, terms) for by in near})
    first = summed(terms.reshape(n_cols, sub, slab), COLS)
    first_pieces = spread_z(first)
    first_out = lax.all_gather(solution_piece(first), COLS, axis=0, tiled=False)
    first_all = lax.all_gather(first_pieces, "x", axis=0, tiled=False)

    terms = apply_matrix(where_z, below, first_pieces, n_y)
    own_0.update({by: moved(trail_0, by, terms) for by in near})
    second_rhs = rhs[width:] - summed(terms, "y")
    held = [own_0[by] for by in near] + [own_1[by] for by in near]
    second_rhs, *held = lax.optimization_barrier((second_rhs, *held))
    own_0.update(zip(near, held[: len(near)]))
    own_1.update(zip(near, held[len(near) :]))
    second_pieces = spread_z(second_rhs)

    terms = apply_matrix(where_z, inverse_1, second_pieces, n_y)
    own_0[far] = moved(trail_0, far, terms)
    second, first_out, own_0[far], own_1[far] = lax.optimization_barrier(
        (summed(terms, "y"), first_out, own_0[far], own_1[far])
    )
    own_0, own_1 = ([own[by] for by in range(n_z)] for own in (own_0, own_1))
    other_0 = [shift(v, "core", 1) for v in own_0]
    other_1 = [shift(v, "core", 1) for v in own_1]

    trail_owner = col // n_z * n_z + jnp.arange(n_z, dtype=jnp.int32)
    slab_order = (jnp.arange(n_x, dtype=jnp.int32) * n_core + core)[:, None] * slab
    list_order = (slab_order + jnp.arange(slab, dtype=jnp.int32)[None, :]).reshape(-1)
    to_lists = (
        (jnp.take(slots_of, list_order)[None, None, :] == slot_range[None, :, None])
        & (jnp.take(owners, list_order)[None, None, :] == trail_owner[:, None, None])
    ).astype(BF16)
    base = apply_trail(where_z, own_0, other_0, width, first_all, to_lists, True)

    piece = solution_piece(second)
    piece = jnp.stack([piece] + [shift(piece, "z", by) for by in range(1, n_z)])
    second_out = [piece] + [shift(piece, "y", by) for by in range(1, n_y)]
    second_all = spread(second, ("x", "z")).reshape(n_x, n_z, n_core, quarter, slab)
    terms = apply_trail(where_z, own_1, other_1, width, second_all, base, False)
    terms = after(terms, *second_out)
    total = summed(terms, "y").reshape(n_core, trail_blocks, quarter, slab)
    kept, given = total[0], total[1]
    got = shift(given, "core", 1)
    pair = jnp.where(core == 0, jnp.stack([kept, got]), jnp.stack([got, kept]))
    pair = pair.reshape(n_core, trail_blocks, quarter, n_z // n_core, run_len).transpose(0, 3, 1, 2, 4)
    out = exchange(pair.reshape(n_z, trail_blocks, quarter, run_len), "z")
    trail_out = out.transpose(1, 0, 2, 3).reshape(trail_blocks, block_rows, run_len)
    first_out = first_out.reshape(n_y, n_z, quarter, n_core * slab)
    return as_rows(jnp.stack([y_at, z_at]).astype(jnp.int32), first_out, second_out), trail_out


def solution(mesh):
    n_rows, n_cols = mesh.devices.shape
    side = int(round(n_cols**0.5))
    mesh = Mesh(mesh.devices.reshape(n_rows // 2, 2, side, n_cols // side), ROWS + COLS)
    return jax.shard_map(
        body,
        mesh=mesh,
        in_specs=(
            P(),
            P(None, ROWS, COLS),
            P(None, ROWS, COLS),
            P(ROWS, COLS),
            P(None, None, ROWS, COLS),
        ),
        out_specs=(P(None, ROWS, None), P(None, ROWS, COLS)),
        check_vma=False,
    )
```

```python
import functools

import jax
import jax.numpy as jnp
from jax import lax
from jax.experimental import pallas as pl
from jax.experimental.pallas import tpu as pltpu
from jax.sharding import Mesh
from jax.sharding import PartitionSpec as P

NCELL = 65536
ROWS = ("x", "core")
COLS = ("y", "z")
HIGHEST = lax.Precision.HIGHEST
F32 = jnp.float32
BF16 = jnp.bfloat16
SMEM = pl.BlockSpec(memory_space=pltpu.SMEM)


def dot(a, b, dims, precision):
    return lax.dot_general(a, b, (dims, ((), ())), precision=precision, preferred_element_type=F32)


def shift(value, axis, by):
    size = lax.axis_size(axis)
    return lax.ppermute(value, axis, [(i, (i + by) % size) for i in range(size)])


def exchange(value, axes):
    return lax.all_to_all(value, axes, 0, 0, tiled=True)


def spread(value, axes):
    return exchange(jnp.broadcast_to(value[None], (lax.axis_size(axes), *value.shape)), axes)


def split(value):
    high = value.astype(BF16)
    return high, (value - high.astype(F32)).astype(BF16)


def mul(a, b):
    f = lambda u, v: jnp.dot(u, v, preferred_element_type=F32)
    return f(a[0], b[0]) + (f(a[0], b[1]) + f(a[1], b[0]))


def band_rows(ref, lead, at, by, n_z):
    source = lax.rem(at + n_z - by, n_z)
    per = n_z // 2
    quarters = [ref[(*lead, per * lax.rem(source, 2) + i, source // 2)] for i in range(per)]
    return jnp.concatenate(quarters, axis=0)


def product_kernel(n_z, at_ref, matrix_ref, operand_ref, out_ref):
    width = matrix_ref.shape[1] // n_z
    slab = operand_ref.shape[-1]
    total = None
    for by in range(n_z):
        high, low = split(band_rows(operand_ref, (), at_ref[0], by, n_z))
        left = split(matrix_ref[:, by * width : (by + 1) * width])
        both = jnp.dot(left[0], jnp.concatenate([high, low], axis=1), preferred_element_type=F32)
        term = both[:, :slab] + (both[:, slab:] + jnp.dot(left[1], high, preferred_element_type=F32))
        total = term if total is None else total + term
    out_ref[...] = total.reshape(out_ref.shape)


def first_kernel(n_z, n_core, matrix_ref, operand_ref, out_ref):
    high, low = split(operand_ref[...])
    slab = operand_ref.shape[-1]
    left = split(matrix_ref[...])
    both = jnp.dot(left[0], jnp.concatenate([high, low], axis=1), preferred_element_type=F32)
    total = both[:, :slab] + (both[:, slab:] + jnp.dot(left[1], high, preferred_element_type=F32))
    quarter = out_ref.shape[-2]
    for k in range(n_core):
        for z in range(n_z):
            at = (k * n_z + z) * quarter
            out_ref[0, z, k] = total[at : at + quarter]


def apply_first(matrix, operand, n_y, n_z, n_core):
    rows, width = matrix.shape
    slab = operand.shape[1]
    quarter = rows // (n_y * n_z * n_core)
    return pl.pallas_call(
        functools.partial(first_kernel, n_z, n_core),
        grid=(n_y,),
        in_specs=[
            pl.BlockSpec((rows // n_y, width), lambda i: (i, 0)),
            pl.BlockSpec(operand.shape, lambda i: (0, 0)),
        ],
        out_specs=pl.BlockSpec((1, n_z, n_core, quarter, slab), lambda i: (i, 0, 0, 0, 0)),
        out_shape=jax.ShapeDtypeStruct((n_y, n_z, n_core, quarter, slab), F32),
        cost_estimate=pl.CostEstimate(
            flops=6 * rows * width * slab, bytes_accessed=4 * rows * width, transcendentals=0
        ),
    )(matrix, operand)


def apply_matrix(at_z, matrix, pieces, n_y):
    rows, band = matrix.shape
    slab = pieces.shape[-1]
    return pl.pallas_call(
        functools.partial(product_kernel, pieces.shape[0]),
        grid=(2,),
        in_specs=[
            SMEM,
            pl.BlockSpec((rows // 2, band), lambda i: (i, 0)),
            pl.BlockSpec(pieces.shape, lambda i: (0, 0, 0, 0)),
        ],
        out_specs=pl.BlockSpec((n_y // 2, rows // n_y, slab), lambda i: (i, 0, 0)),
        out_shape=jax.ShapeDtypeStruct((n_y, rows // n_y, slab), F32),
        cost_estimate=pl.CostEstimate(
            flops=6 * rows * band * slab, bytes_accessed=4 * rows * band, transcendentals=0
        ),
    )(at_z, matrix, pieces)


def trail_kernel(n_z, with_gram, at_ref, lists_ref, *refs):
    factor = refs[: 2 * n_z]
    refs = refs[2 * n_z :]
    gram = refs[: 2 * n_z] if with_gram else ()
    start_ref, out_ref, high_ref, low_ref, chosen_ref = refs[len(gram) :]
    n_x, at_z = lists_ref.shape[0], at_ref[0]
    width = factor[0].shape[-1]
    slots = start_ref.shape[1] if with_gram else 0
    slab = out_ref.shape[-1]

    @pl.when(pl.program_id(0) == 0)
    def _():
        for by in range(n_z):
            for i in range(n_x):
                rows = band_rows(lists_ref, (i,), at_z, by, n_z)
                into = slice(by * width, (by + 1) * width), slice(i * slab, (i + 1) * slab)
                high_ref[into], low_ref[into] = split(rows)
            if with_gram:
                chosen_ref[by * slots : (by + 1) * slots, :] = start_ref[lax.rem(at_z + n_z - by, n_z)]

    def left(pieces):
        sides = [jnp.concatenate([v[0] for v in pieces[side * n_z :][:n_z]], axis=1) for side in range(2)]
        return split(jnp.concatenate(sides, axis=0))

    total = mul(left(factor), (high_ref[...], low_ref[...]))
    if with_gram:
        high, low = left(gram)
        chosen = chosen_ref[...]
        placed = jnp.dot(high, chosen, preferred_element_type=F32) + jnp.dot(low, chosen, preferred_element_type=F32)
        total = placed - total
    half = total.shape[0] // 2
    for i in range(n_x):
        for side in range(2):
            part = total[side * half : (side + 1) * half, i * slab : (i + 1) * slab]
            out_ref[i, side, 0] = part if with_gram else start_ref[i, side, 0] - part


def apply_trail(where, own, other, width, lists, start, with_gram):
    n_z = len(own)
    blocks, quarter, depth = own[0].shape
    slots = depth - width
    n_x, slab = lists.shape[0], lists.shape[-1]
    whole = lambda v: pl.BlockSpec(v.shape, lambda *_: (0,) * v.ndim)
    part = pl.BlockSpec((1, quarter, width), lambda t: (t, 0, 0))
    ends = pl.BlockSpec((n_x, 2, 1, quarter, slab), lambda t: (0, 0, t, 0, 0))
    pieces = [*own, *other]
    specs = [SMEM, whole(lists)] + [part] * (2 * n_z)
    args = [where, lists, *pieces]
    if with_gram:
        specs += [pl.BlockSpec((1, quarter, slots), lambda t: (t, 0, width // slots))] * (2 * n_z)
        args += pieces
    band, n_list = n_z * width, n_x * slab
    return pl.pallas_call(
        functools.partial(trail_kernel, n_z, with_gram),
        grid=(blocks,),
        in_specs=specs + [whole(start) if with_gram else ends],
        out_specs=ends,
        out_shape=jax.ShapeDtypeStruct((n_x, 2, blocks, quarter, slab), F32),
        scratch_shapes=[
            pltpu.VMEM((band, n_list), BF16),
            pltpu.VMEM((band, n_list), BF16),
            pltpu.VMEM((n_z * max(slots, 16), n_list), BF16),
        ],
        cost_estimate=pl.CostEstimate(
            flops=12 * blocks * quarter * band * n_list, bytes_accessed=10 * 2**20, transcendentals=0
        ),
    )(*args, start)


def rows_kernel(pieces_ref, out_ref):
    n_y, _, n_panels, _, wide = pieces_ref.shape
    for y in range(n_y):
        for panel in range(n_panels):
            out_ref[panel, :, y * wide : (y + 1) * wide] = pieces_ref[y, 0, panel]


def as_rows(pieces):
    n_y, n_z, n_panels, quarter, wide = pieces.shape
    return pl.pallas_call(
        rows_kernel,
        grid=(n_z,),
        in_specs=[pl.BlockSpec((n_y, 1, n_panels, quarter, wide), lambda i: (0, i, 0, 0, 0))],
        out_specs=pl.BlockSpec((n_panels, quarter, n_y * wide), lambda i: (0, i, 0)),
        out_shape=jax.ShapeDtypeStruct((n_panels, n_z * quarter, n_y * wide), F32),
        cost_estimate=pl.CostEstimate(flops=0, bytes_accessed=8 * 2**20, transcendentals=0),
    )(pieces)


def after(value, *others):
    return lax.optimization_barrier((value, *others))[0]


def body(cells, gram_slots, diag_inverse, lower_block, trail_factor):
    n_x, n_core, n_y, n_z = (lax.axis_size(a) for a in ROWS + COLS)
    n_rows, n_cols = n_x * n_core, n_y * n_z
    col = lax.axis_index(COLS)
    row = lax.axis_index(ROWS)
    core = lax.axis_index("core")
    z_at = lax.axis_index("z")
    list_len = cells.shape[0]
    run_len = list_len // n_cols
    slab = list_len // n_rows
    runs_in_slab = slab // run_len
    block_rows = gram_slots.shape[1]
    capacity = gram_slots.shape[2]
    per_run = capacity // n_cols
    slab_slots = runs_in_slab * per_run
    width = diag_inverse.shape[2]
    trail_blocks = trail_factor.shape[0]
    quarter = block_rows // n_z
    sub = n_core * quarter

    owners = cells // (NCELL // n_cols)
    onehot = (owners[:, None] == jnp.arange(n_cols, dtype=jnp.int32)[None, :]).astype(jnp.int32)
    blocked = onehot.reshape(n_cols, run_len, n_cols)
    lower = jnp.tril(jnp.ones((run_len, run_len), F32), -1)
    in_run = jnp.einsum("ij,bjo->bio", lower, blocked.astype(F32)).astype(jnp.int32)
    run_total = jnp.sum(blocked, axis=1)
    runs = jnp.arange(n_cols)
    before = jnp.sum(jnp.where(runs[:, None, None] > runs[None, :, None], run_total[None, :, :], 0), axis=1)
    pair_rank = jnp.sum(in_run * blocked, axis=2).reshape(list_len)
    slots_of = pair_rank + jnp.sum(before[:, None, :] * blocked, axis=2).reshape(list_len)
    mine = owners == col
    position = jnp.arange(list_len, dtype=jnp.int32) // run_len * per_run + pair_rank
    slot_range = jnp.arange(capacity, dtype=jnp.int32)
    to_list = ((slots_of[None, :] == slot_range[:, None]) & mine[None, :]).astype(F32)
    to_runs = dot(
        ((position[None, :] == slot_range[:, None]) & mine[None, :]).astype(F32),
        to_list,
        ((1,), (1,)),
        lax.Precision.DEFAULT,
    )

    def moved(cut, by, ready=None):
        value = cut((z_at + by) % n_z)
        return shift(value if ready is None else after(value, ready), "z", by) if by else value

    def quarters(cut):
        return [moved(cut, by) for by in range(n_z)]

    def rows_at(matrix, at):
        return lax.dynamic_slice_in_dim(matrix, at * quarter, quarter, matrix.ndim - 2)

    def all_rows(pieces):
        return lax.all_gather(jnp.concatenate(pieces, axis=1), ROWS, axis=0, tiled=True)

    inverse_0 = lax.all_gather(diag_inverse[0], ROWS, axis=0, tiled=True)

    outgoing = lax.dot_general(
        to_runs, gram_slots[0:2], (((1,), (2,)), ((), ())), precision=HIGHEST, preferred_element_type=F32
    )
    blocks = after(jnp.stack([lower_block, diag_inverse[1]]), outgoing)
    pieces = quarters(lambda at: rows_at(blocks, at))
    slab_gram = exchange(outgoing.reshape(n_rows, slab_slots, 2, block_rows), ROWS)
    pieces = list(lax.optimization_barrier((*pieces, slab_gram)))[:-1]
    below, inverse_1 = (all_rows([v[i] for v in pieces]) for i in range(2))
    by_width = slab_gram[:, :, 0].reshape(n_rows, slab_slots, block_rows // width, width)
    by_width = by_width.transpose(0, 2, 1, 3).reshape(n_cols, slab_slots, width)
    by_sub = slab_gram[:, :, 1].reshape(n_y, n_core, slab_slots, n_z, quarter).transpose(0, 3, 2, 1, 4)
    by_sub = by_sub.reshape(n_cols, slab_slots, sub)
    sub_gram = exchange(jnp.concatenate([by_width, by_sub], axis=2), COLS)
    slab_owner = lax.dynamic_slice_in_dim(owners, row * slab, slab)
    slab_rank = lax.dynamic_slice_in_dim(pair_rank, row * slab, slab)
    slab_slot = jnp.arange(slab, dtype=jnp.int32) // run_len * per_run + slab_rank
    from_owner = (
        jnp.arange(n_cols * slab_slots, dtype=jnp.int32)[:, None] == (slab_owner * slab_slots + slab_slot)[None, :]
    ).astype(F32)
    rhs = dot(sub_gram.reshape(n_cols * slab_slots, width + sub), from_owner, ((0,), (0,)), HIGHEST)

    where_z = z_at.astype(jnp.int32).reshape(1)

    def spread_z(block):
        return spread(block, "z").reshape(n_z, n_core, quarter, slab)

    def summed(terms, axes):
        return jnp.sum(exchange(terms, axes), axis=0)

    axes = ROWS + COLS
    sizes = (n_x, n_core, n_y, n_z)

    def device(x, k, y, z):
        return ((x * n_core + k) * n_y + y) * n_z + z

    def solution_piece(block):
        pieces = block.reshape(n_core, quarter, slab)
        arrived = []
        for m in range(n_core):
            to = [
                (device(x, k, y, z), device(y, k ^ m, x, z))
                for x in range(n_x)
                for k in range(n_core)
                for y in range(n_y)
                for z in range(n_z)
            ]
            arrived.append(lax.ppermute(lax.dynamic_index_in_dim(pieces, core ^ m, 0, keepdims=False), axes, to))
        return jnp.where(core == 0, jnp.concatenate(arrived, axis=1), jnp.concatenate(arrived[::-1], axis=1))

    def trail_0(at):
        return jnp.concatenate([rows_at(trail_factor[:, 0], at), rows_at(gram_slots[2:], at)], axis=2)

    def trail_1(at):
        return rows_at(trail_factor[:, 1], at)

    far = n_z // 2
    near = [by for by in range(1, n_z) if by != far]
    own_0, own_1 = {0: trail_0(z_at)}, {0: trail_1(z_at)}
    terms = apply_first(inverse_0, rhs[:width], n_y, n_z, n_core)
    own_1[far] = moved(trail_1, far, slab_gram)
    own_1.update({by: moved(trail_1, by, terms) for by in near})
    first = after(summed(terms.reshape(n_cols, sub, slab), COLS), *own_1.values())
    first_pieces = spread_z(first)
    first_all = lax.all_gather(first_pieces, "x", axis=0, tiled=False)
    first_piece = solution_piece(first)

    terms = apply_matrix(where_z, below, first_pieces, n_y)
    own_0.update({by: moved(trail_0, by, terms) for by in near})
    second_rhs = after(rhs[width:] - summed(terms, "y"), first_piece, *own_0.values())
    second_pieces = spread_z(second_rhs)

    terms = apply_matrix(where_z, inverse_1, second_pieces, n_y)
    own_0[far] = moved(trail_0, far, terms)
    own_0, own_1 = ([own[by] for by in range(n_z)] for own in (own_0, own_1))
    other_0 = [shift(v, "core", 1) for v in own_0]
    other_1 = [shift(v, "core", 1) for v in own_1]

    trail_owner = col // n_z * n_z + jnp.arange(n_z, dtype=jnp.int32)
    slab_order = (jnp.arange(n_x, dtype=jnp.int32) * n_core + core)[:, None] * slab
    list_order = (slab_order + jnp.arange(slab, dtype=jnp.int32)[None, :]).reshape(-1)
    to_lists = (
        (jnp.take(slots_of, list_order)[None, None, :] == slot_range[None, :, None])
        & (jnp.take(owners, list_order)[None, None, :] == trail_owner[:, None, None])
    ).astype(BF16)
    base = apply_trail(where_z, own_0, other_0, width, first_all, to_lists, True)

    second = after(summed(terms, "y"), own_0[far])
    solved = lax.all_gather(jnp.stack([first_piece, solution_piece(second)]), COLS, axis=0, tiled=False)
    second_all = spread(second, ("x", "z")).reshape(n_x, n_z, n_core, quarter, slab)
    terms = apply_trail(where_z, own_1, other_1, width, second_all, base, False)
    total = summed(terms, "y").reshape(n_core, trail_blocks, quarter, slab)
    kept, given = total[0], total[1]
    got = shift(given, "core", 1)
    pair = jnp.where(core == 0, jnp.stack([kept, got]), jnp.stack([got, kept]))
    pair = pair.reshape(n_core, trail_blocks, quarter, n_z // n_core, run_len).transpose(0, 3, 1, 2, 4)
    out = exchange(pair.reshape(n_z, trail_blocks, quarter, run_len), "z")
    trail_out = out.transpose(1, 0, 2, 3).reshape(trail_blocks, block_rows, run_len)
    return as_rows(solved.reshape(n_y, n_z, 2, quarter, n_core * slab)), trail_out


def solution(mesh):
    n_rows, n_cols = mesh.devices.shape
    side = int(round(n_cols**0.5))
    mesh = Mesh(mesh.devices.reshape(n_rows // 2, 2, side, n_cols // side), ROWS + COLS)
    return jax.shard_map(
        body,
        mesh=mesh,
        in_specs=(
            P(),
            P(None, ROWS, COLS),
            P(None, ROWS, COLS),
            P(ROWS, COLS),
            P(None, None, ROWS, COLS),
        ),
        out_specs=(P(None, ROWS, None), P(None, ROWS, COLS)),
        check_vma=False,
    )
```

```python
import functools

import jax
import jax.numpy as jnp
from jax import lax
from jax.experimental import pallas as pl
from jax.experimental.pallas import tpu as pltpu
from jax.sharding import Mesh
from jax.sharding import PartitionSpec as P

NCELL = 65536
ROWS = ("x", "core")
COLS = ("y", "z")
HIGHEST = lax.Precision.HIGHEST
F32 = jnp.float32
BF16 = jnp.bfloat16
SMEM = pl.BlockSpec(memory_space=pltpu.SMEM)


def dot(a, b, dims, precision):
    return lax.dot_general(a, b, (dims, ((), ())), precision=precision, preferred_element_type=F32)


def shift(value, axis, by):
    size = lax.axis_size(axis)
    return lax.ppermute(value, axis, [(i, (i + by) % size) for i in range(size)])


def exchange(value, axes):
    return lax.all_to_all(value, axes, 0, 0, tiled=True)


def spread(value, axes):
    return exchange(jnp.broadcast_to(value[None], (lax.axis_size(axes), *value.shape)), axes)


def split(value):
    high = value.astype(BF16)
    return high, (value - high.astype(F32)).astype(BF16)


def mul(a, b):
    f = lambda u, v: jnp.dot(u, v, preferred_element_type=F32)
    return f(a[0], b[0]) + (f(a[0], b[1]) + f(a[1], b[0]))


def band_rows(ref, lead, at, by, n_z):
    source = lax.rem(at + n_z - by, n_z)
    per = n_z // 2
    quarters = [ref[(*lead, per * lax.rem(source, 2) + i, source // 2)] for i in range(per)]
    return jnp.concatenate(quarters, axis=0)


def product_kernel(n_z, at_ref, matrix_ref, operand_ref, out_ref):
    width = matrix_ref.shape[1] // n_z
    slab = operand_ref.shape[-1]
    total = None
    for by in range(n_z):
        high, low = split(band_rows(operand_ref, (), at_ref[0], by, n_z))
        left = split(matrix_ref[:, by * width : (by + 1) * width])
        both = jnp.dot(left[0], jnp.concatenate([high, low], axis=1), preferred_element_type=F32)
        term = both[:, :slab] + (both[:, slab:] + jnp.dot(left[1], high, preferred_element_type=F32))
        total = term if total is None else total + term
    out_ref[...] = total.reshape(out_ref.shape)


def first_kernel(n_z, n_core, matrix_ref, operand_ref, out_ref):
    high, low = split(operand_ref[...])
    slab = operand_ref.shape[-1]
    left = split(matrix_ref[...])
    both = jnp.dot(left[0], jnp.concatenate([high, low], axis=1), preferred_element_type=F32)
    total = both[:, :slab] + (both[:, slab:] + jnp.dot(left[1], high, preferred_element_type=F32))
    quarter = out_ref.shape[-2]
    for k in range(n_core):
        for z in range(n_z):
            at = (k * n_z + z) * quarter
            out_ref[0, z, k] = total[at : at + quarter]


def apply_first(matrix, operand, n_y, n_z, n_core):
    rows, width = matrix.shape
    slab = operand.shape[1]
    quarter = rows // (n_y * n_z * n_core)
    return pl.pallas_call(
        functools.partial(first_kernel, n_z, n_core),
        grid=(n_y,),
        in_specs=[
            pl.BlockSpec((rows // n_y, width), lambda i: (i, 0)),
            pl.BlockSpec(operand.shape, lambda i: (0, 0)),
        ],
        out_specs=pl.BlockSpec((1, n_z, n_core, quarter, slab), lambda i: (i, 0, 0, 0, 0)),
        out_shape=jax.ShapeDtypeStruct((n_y, n_z, n_core, quarter, slab), F32),
        cost_estimate=pl.CostEstimate(
            flops=6 * rows * width * slab, bytes_accessed=4 * rows * width, transcendentals=0
        ),
    )(matrix, operand)


def apply_matrix(at_z, matrix, pieces, n_y):
    rows, band = matrix.shape
    slab = pieces.shape[-1]
    return pl.pallas_call(
        functools.partial(product_kernel, pieces.shape[0]),
        grid=(2,),
        in_specs=[
            SMEM,
            pl.BlockSpec((rows // 2, band), lambda i: (i, 0)),
            pl.BlockSpec(pieces.shape, lambda i: (0, 0, 0, 0)),
        ],
        out_specs=pl.BlockSpec((n_y // 2, rows // n_y, slab), lambda i: (i, 0, 0)),
        out_shape=jax.ShapeDtypeStruct((n_y, rows // n_y, slab), F32),
        cost_estimate=pl.CostEstimate(
            flops=6 * rows * band * slab, bytes_accessed=4 * rows * band, transcendentals=0
        ),
    )(at_z, matrix, pieces)


def trail_kernel(n_z, with_gram, at_ref, lists_ref, *refs):
    factor = refs[: 2 * n_z]
    refs = refs[2 * n_z :]
    gram = refs[: 2 * n_z] if with_gram else ()
    start_ref, out_ref, high_ref, low_ref, chosen_ref = refs[len(gram) :]
    n_x, at_z = lists_ref.shape[0], at_ref[0]
    width = factor[0].shape[-1]
    slots = start_ref.shape[1] if with_gram else 0
    slab = out_ref.shape[-1]

    @pl.when(pl.program_id(0) == 0)
    def _():
        for by in range(n_z):
            for i in range(n_x):
                rows = band_rows(lists_ref, (i,), at_z, by, n_z)
                into = slice(by * width, (by + 1) * width), slice(i * slab, (i + 1) * slab)
                high_ref[into], low_ref[into] = split(rows)
            if with_gram:
                chosen_ref[by * slots : (by + 1) * slots, :] = start_ref[lax.rem(at_z + n_z - by, n_z)]

    def left(pieces):
        sides = [jnp.concatenate([v[0] for v in pieces[side * n_z :][:n_z]], axis=1) for side in range(2)]
        return split(jnp.concatenate(sides, axis=0))

    total = mul(left(factor), (high_ref[...], low_ref[...]))
    if with_gram:
        high, low = left(gram)
        chosen = chosen_ref[...]
        placed = jnp.dot(high, chosen, preferred_element_type=F32) + jnp.dot(low, chosen, preferred_element_type=F32)
        total = placed - total
    half = total.shape[0] // 2
    for i in range(n_x):
        for side in range(2):
            part = total[side * half : (side + 1) * half, i * slab : (i + 1) * slab]
            out_ref[i, side, 0] = part if with_gram else start_ref[i, side, 0] - part


def apply_trail(where, own, other, width, lists, start, with_gram):
    n_z = len(own)
    blocks, quarter, depth = own[0].shape
    slots = depth - width
    n_x, slab = lists.shape[0], lists.shape[-1]
    whole = lambda v: pl.BlockSpec(v.shape, lambda *_: (0,) * v.ndim)
    part = pl.BlockSpec((1, quarter, width), lambda t: (t, 0, 0))
    ends = pl.BlockSpec((n_x, 2, 1, quarter, slab), lambda t: (0, 0, t, 0, 0))
    pieces = [*own, *other]
    specs = [SMEM, whole(lists)] + [part] * (2 * n_z)
    args = [where, lists, *pieces]
    if with_gram:
        specs += [pl.BlockSpec((1, quarter, slots), lambda t: (t, 0, width // slots))] * (2 * n_z)
        args += pieces
    band, n_list = n_z * width, n_x * slab
    return pl.pallas_call(
        functools.partial(trail_kernel, n_z, with_gram),
        grid=(blocks,),
        in_specs=specs + [whole(start) if with_gram else ends],
        out_specs=ends,
        out_shape=jax.ShapeDtypeStruct((n_x, 2, blocks, quarter, slab), F32),
        scratch_shapes=[
            pltpu.VMEM((band, n_list), BF16),
            pltpu.VMEM((band, n_list), BF16),
            pltpu.VMEM((n_z * max(slots, 16), n_list), BF16),
        ],
        cost_estimate=pl.CostEstimate(
            flops=12 * blocks * quarter * band * n_list, bytes_accessed=10 * 2**20, transcendentals=0
        ),
    )(*args, start)


def rows_kernel(pieces_ref, out_ref):
    n_y, _, n_panels, _, wide = pieces_ref.shape
    for y in range(n_y):
        for panel in range(n_panels):
            out_ref[panel, :, y * wide : (y + 1) * wide] = pieces_ref[y, 0, panel]


def as_rows(pieces):
    n_y, n_z, n_panels, quarter, wide = pieces.shape
    return pl.pallas_call(
        rows_kernel,
        grid=(n_z,),
        in_specs=[pl.BlockSpec((n_y, 1, n_panels, quarter, wide), lambda i: (0, i, 0, 0, 0))],
        out_specs=pl.BlockSpec((n_panels, quarter, n_y * wide), lambda i: (0, i, 0)),
        out_shape=jax.ShapeDtypeStruct((n_panels, n_z * quarter, n_y * wide), F32),
        cost_estimate=pl.CostEstimate(flops=0, bytes_accessed=8 * 2**20, transcendentals=0),
    )(pieces)


def after(value, *others):
    return lax.optimization_barrier((value, *others))[0]


def body(cells, gram_slots, diag_inverse, lower_block, trail_factor):
    n_x, n_core, n_y, n_z = (lax.axis_size(a) for a in ROWS + COLS)
    n_rows, n_cols = n_x * n_core, n_y * n_z
    col = lax.axis_index(COLS)
    row = lax.axis_index(ROWS)
    core = lax.axis_index("core")
    z_at = lax.axis_index("z")
    list_len = cells.shape[0]
    run_len = list_len // n_cols
    slab = list_len // n_rows
    runs_in_slab = slab // run_len
    block_rows = gram_slots.shape[1]
    capacity = gram_slots.shape[2]
    per_run = capacity // n_cols
    slab_slots = runs_in_slab * per_run
    width = diag_inverse.shape[2]
    trail_blocks = trail_factor.shape[0]
    quarter = block_rows // n_z
    sub = n_core * quarter

    owners = cells // (NCELL // n_cols)
    onehot = (owners[:, None] == jnp.arange(n_cols, dtype=jnp.int32)[None, :]).astype(jnp.int32)
    blocked = onehot.reshape(n_cols, run_len, n_cols)
    lower = jnp.tril(jnp.ones((run_len, run_len), F32), -1)
    in_run = jnp.einsum("ij,bjo->bio", lower, blocked.astype(F32)).astype(jnp.int32)
    run_total = jnp.sum(blocked, axis=1)
    runs = jnp.arange(n_cols)
    before = jnp.sum(jnp.where(runs[:, None, None] > runs[None, :, None], run_total[None, :, :], 0), axis=1)
    pair_rank = jnp.sum(in_run * blocked, axis=2).reshape(list_len)
    slots_of = pair_rank + jnp.sum(before[:, None, :] * blocked, axis=2).reshape(list_len)
    mine = owners == col
    position = jnp.arange(list_len, dtype=jnp.int32) // run_len * per_run + pair_rank
    slot_range = jnp.arange(capacity, dtype=jnp.int32)
    to_list = ((slots_of[None, :] == slot_range[:, None]) & mine[None, :]).astype(F32)
    to_runs = dot(
        ((position[None, :] == slot_range[:, None]) & mine[None, :]).astype(F32),
        to_list,
        ((1,), (1,)),
        lax.Precision.DEFAULT,
    )

    def moved(cut, by, ready=None):
        value = cut((z_at + by) % n_z)
        return shift(value if ready is None else after(value, ready), "z", by) if by else value

    def quarters(cut):
        return [moved(cut, by) for by in range(n_z)]

    def rows_at(matrix, at):
        return lax.dynamic_slice_in_dim(matrix, at * quarter, quarter, matrix.ndim - 2)

    def all_rows(pieces):
        return lax.all_gather(jnp.concatenate(pieces, axis=1), ROWS, axis=0, tiled=True)

    inverse_0 = lax.all_gather(diag_inverse[0], ROWS, axis=0, tiled=True)

    outgoing = lax.dot_general(
        to_runs, gram_slots[0:2], (((1,), (2,)), ((), ())), precision=HIGHEST, preferred_element_type=F32
    )
    blocks = after(jnp.stack([lower_block, diag_inverse[1]]), outgoing)
    pieces = quarters(lambda at: rows_at(blocks, at))
    slab_gram = exchange(outgoing.reshape(n_rows, slab_slots, 2, block_rows), ROWS)
    pieces = list(lax.optimization_barrier((*pieces, slab_gram)))[:-1]
    below, inverse_1 = (all_rows([v[i] for v in pieces]) for i in range(2))
    by_width = slab_gram[:, :, 0].reshape(n_rows, slab_slots, block_rows // width, width)
    by_width = by_width.transpose(0, 2, 1, 3).reshape(n_cols, slab_slots, width)
    by_sub = slab_gram[:, :, 1].reshape(n_y, n_core, slab_slots, n_z, quarter).transpose(0, 3, 2, 1, 4)
    by_sub = by_sub.reshape(n_cols, slab_slots, sub)
    sub_gram = exchange(jnp.concatenate([by_width, by_sub], axis=2), COLS)
    far_piece = moved(lambda at: rows_at(trail_factor[:, 1], at), n_z // 2, slab_gram)
    sub_gram, far_piece = lax.optimization_barrier((sub_gram, far_piece))
    slab_owner = lax.dynamic_slice_in_dim(owners, row * slab, slab)
    slab_rank = lax.dynamic_slice_in_dim(pair_rank, row * slab, slab)
    slab_slot = jnp.arange(slab, dtype=jnp.int32) // run_len * per_run + slab_rank
    from_owner = (
        jnp.arange(n_cols * slab_slots, dtype=jnp.int32)[:, None] == (slab_owner * slab_slots + slab_slot)[None, :]
    ).astype(F32)
    rhs = dot(sub_gram.reshape(n_cols * slab_slots, width + sub), from_owner, ((0,), (0,)), HIGHEST)

    where_z = z_at.astype(jnp.int32).reshape(1)

    def spread_z(block):
        return spread(block, "z").reshape(n_z, n_core, quarter, slab)

    def summed(terms, axes):
        return jnp.sum(exchange(terms, axes), axis=0)

    axes = ROWS + COLS
    sizes = (n_x, n_core, n_y, n_z)

    def device(x, k, y, z):
        return ((x * n_core + k) * n_y + y) * n_z + z

    def solution_piece(block):
        pieces = block.reshape(n_core, quarter, slab)
        arrived = []
        for m in range(n_core):
            to = [
                (device(x, k, y, z), device(y, k ^ m, x, z))
                for x in range(n_x)
                for k in range(n_core)
                for y in range(n_y)
                for z in range(n_z)
            ]
            arrived.append(lax.ppermute(lax.dynamic_index_in_dim(pieces, core ^ m, 0, keepdims=False), axes, to))
        return jnp.where(core == 0, jnp.concatenate(arrived, axis=1), jnp.concatenate(arrived[::-1], axis=1))

    def trail_0(at):
        return jnp.concatenate([rows_at(trail_factor[:, 0], at), rows_at(gram_slots[2:], at)], axis=2)

    def trail_1(at):
        return rows_at(trail_factor[:, 1], at)

    far = n_z // 2
    near = [by for by in range(1, n_z) if by != far]
    own_0, own_1 = {0: trail_0(z_at)}, {0: trail_1(z_at)}
    terms = apply_first(inverse_0, rhs[:width], n_y, n_z, n_core)
    own_1[far] = far_piece
    own_1.update({by: moved(trail_1, by, terms) for by in near})
    first = after(summed(terms.reshape(n_cols, sub, slab), COLS), *own_1.values())
    first_pieces = spread_z(first)
    first_all = lax.all_gather(first_pieces, "x", axis=0, tiled=False)
    first_piece = solution_piece(first)

    terms = apply_matrix(where_z, below, first_pieces, n_y)
    own_0.update({by: moved(trail_0, by, terms) for by in near})
    second_rhs = after(rhs[width:] - summed(terms, "y"), first_piece, *own_0.values())
    second_pieces = spread_z(second_rhs)

    terms = apply_matrix(where_z, inverse_1, second_pieces, n_y)
    own_0[far] = moved(trail_0, far, terms)
    own_0, own_1 = ([own[by] for by in range(n_z)] for own in (own_0, own_1))
    other_0 = [shift(v, "core", 1) for v in own_0]
    other_1 = [shift(v, "core", 1) for v in own_1]

    trail_owner = col // n_z * n_z + jnp.arange(n_z, dtype=jnp.int32)
    slab_order = (jnp.arange(n_x, dtype=jnp.int32) * n_core + core)[:, None] * slab
    list_order = (slab_order + jnp.arange(slab, dtype=jnp.int32)[None, :]).reshape(-1)
    to_lists = (
        (jnp.take(slots_of, list_order)[None, None, :] == slot_range[None, :, None])
        & (jnp.take(owners, list_order)[None, None, :] == trail_owner[:, None, None])
    ).astype(BF16)
    base = apply_trail(where_z, own_0, other_0, width, first_all, to_lists, True)

    second = after(summed(terms, "y"), own_0[far])
    solved = lax.all_gather(jnp.stack([first_piece, solution_piece(second)]), COLS, axis=0, tiled=False)
    second_all = spread(second, ("x", "z")).reshape(n_x, n_z, n_core, quarter, slab)
    terms = apply_trail(where_z, own_1, other_1, width, second_all, base, False)
    total = summed(terms, "y").reshape(n_core, trail_blocks, quarter, slab)
    kept, given = total[0], total[1]
    got = shift(given, "core", 1)
    pair = jnp.where(core == 0, jnp.stack([kept, got]), jnp.stack([got, kept]))
    pair = pair.reshape(n_core, trail_blocks, quarter, n_z // n_core, run_len).transpose(0, 3, 1, 2, 4)
    out = exchange(pair.reshape(n_z, trail_blocks, quarter, run_len), "z")
    trail_out = out.transpose(1, 0, 2, 3).reshape(trail_blocks, block_rows, run_len)
    return as_rows(solved.reshape(n_y, n_z, 2, quarter, n_core * slab)), trail_out


def solution(mesh):
    n_rows, n_cols = mesh.devices.shape
    side = int(round(n_cols**0.5))
    mesh = Mesh(mesh.devices.reshape(n_rows // 2, 2, side, n_cols // side), ROWS + COLS)
    return jax.shard_map(
        body,
        mesh=mesh,
        in_specs=(
            P(),
            P(None, ROWS, COLS),
            P(None, ROWS, COLS),
            P(ROWS, COLS),
            P(None, None, ROWS, COLS),
        ),
        out_specs=(P(None, ROWS, None), P(None, ROWS, COLS)),
        check_vma=False,
    )
```
